32 devices in a mesh: dom: 8 (over z, y), grp: 4 (over x, core).
Axes of the slice: x: 2, y: 2, z: 4, core: 2. Of those that a mesh axis runs over, the one named last changes fastest.
Arguments:
- a_blocks: bfloat16 [32, 7, 48, 64, 448], P('dom', None, 'grp'), may hold values from -0.25 to 0.25
- prolong: bfloat16 [32, 7, 48, 64, 128], P('dom', None, 'grp'), may hold values from -0.75 to 0.75
- zagg: int32 [32], replicated, may hold values from 0 to 15, as said below
- xlen: int32 [4, 4], replicated, may hold values from 1 to 6, 12 in all within a row
Outputs:
- coarse_operator: bfloat16 [16, 16, 128, 640], P('dom', 'grp')
The draws below stay inside these ranges and needn't reach their ends.
Inputs may be any that keep to these rules, and one draw needn't show every extreme that they name: zagg starts at 0, never falls and rises by 0 or 1 from layer to layer; every run of 4 layers of one index of dom holds exactly 2 layers where a new interval begins, the first layer of all among them.
All inputs are finite; a program needn't handle non-finite values.
Results may differ from the reference program's by a relative error of at most 0.005.
Values may be sent and summed in bfloat16 or wider, within the bound.
No kernel may reach another device: no remote copies, remote signals or barrier semaphores. Data moves between devices by JAX's collectives and lax.ppermute only.
A program may use at most 256 MiB of HBM per device.

```python
import math
import jax
import jax.numpy as jnp
import numpy as np
from jax import lax

B = 64
BC = 128
LX = 12
LY = 7
LZ = 4
NXI = 4
Z = 32
X = 48
N_DOM = 8
N_GRP = 4


def draw_zagg(key, part):
    noise = jax.random.randint(key, (N_DOM, LZ), 0, 1 << 20)
    places = jnp.arange(LZ, dtype=jnp.int32)
    scores = noise * LZ + places[None, :]
    marker = jnp.zeros((N_DOM, LZ), jnp.int32).at[0, 0].set(1)
    scores = jnp.where(marker > 0, -1, scores)
    ranking = jnp.argsort(jnp.argsort(scores, axis=1), axis=1)
    begins = (ranking < LZ // 2).astype(jnp.int32).reshape(-1)
    return (jnp.cumsum(begins) - 1).astype(jnp.int32)


def shard_levels(key, shape, shards, least, largest):
    def one(axis_at, blocks):
        heights = jax.random.uniform(jax.random.fold_in(jax.random.fold_in(key, 6), axis_at), (blocks,), jnp.float32, least / len(shards), largest / len(shards))
        return jnp.repeat(jnp.exp(heights), shape[axis_at] // blocks).reshape((-1,) + (1,) * (len(shape) - axis_at - 1))

    factor_of = one(*shards[0])
    for cut in shards[1:]:
        factor_of = factor_of * one(*cut)
    return factor_of


def length_profile(number_of, total, bound, skew):
    portions = [(1 << 20) // math.isqrt(grade ** skew) + 1 for grade in range(2, number_of + 1)]
    rest, counts = total - bound - (number_of - 1), [1] * (number_of - 1)
    while rest > 0:
        free = [i for i in range(number_of - 1) if counts[i] < bound]
        whole, budget = sum([portions[i] for i in free]), rest
        for i in free:
            addition = min(bound - counts[i], max(1, budget * portions[i] // whole), rest)
            counts[i] = counts[i] + addition
            rest = rest - addition
    return np.array([bound] + counts)


def ragged_sizes(stream_key, number_of, total, limit, slope):
    if number_of == 2:
        one = jax.random.randint(stream_key, (), max(1, total - limit), min(limit, total - 1) + 1)
        return jnp.stack([one, total - one])
    sizes = jnp.asarray(length_profile(number_of, total, limit, slope), jnp.int32)
    pairs = (number_of - 1) // 2
    donor, receiver = sizes[1:1 + 2 * pairs:2], sizes[2:2 + 2 * pairs:2]
    slack = jnp.minimum(donor - 1, limit - receiver)
    passed = jax.random.randint(jax.random.fold_in(stream_key, 1), (pairs,), 0, 1 << 20) % (slack + 1)
    sizes = sizes.at[1:1 + 2 * pairs:2].set(donor - passed).at[2:2 + 2 * pairs:2].set(receiver + passed)
    return sizes[jax.random.permutation(jax.random.fold_in(stream_key, 2), number_of)]


def gaussian(key, dims, scale, most, shards=(), kind=jnp.bfloat16):
    factor_of = shard_levels(key, dims, shards, -0.22, 0.18) if shards else 1.0
    result = jax.random.normal(key, dims, jnp.float32) * scale * factor_of
    return jnp.minimum(jnp.maximum(result, -most), most).astype(kind)


def setup_inputs(seed: int = 0) -> dict:
    keys = jax.random.split(jax.random.key(seed), 5)
    a_blocks = gaussian(keys[0], (Z, LY, X, B, 7 * B), (7 * B) ** -0.5, 0.25, ((0, 8), (2, 4)))
    prolong = gaussian(keys[1], (Z, LY, X, B, BC), B ** -0.5, 0.75, ((0, 8), (2, 4)))
    zagg = draw_zagg(jax.random.fold_in(keys[4], 71), 0)
    xlen = jax.vmap(lambda own: ragged_sizes(own, NXI, LX, LX // 3 + 2, 2))(jax.random.split(keys[3], N_GRP)).reshape((N_GRP, NXI)).astype(jnp.int32)
    return {"a_blocks": a_blocks, "prolong": prolong, "zagg": zagg, "xlen": xlen}


def reference(a_blocks, prolong, zagg, xlen):
    ends = jnp.cumsum(xlen, axis=1)
    columns = jnp.arange(LX, dtype=jnp.int32)
    within = jnp.sum((ends[:, :, None] <= columns[None, None, :]).astype(jnp.int32), axis=1)
    offsets = jnp.arange(N_GRP, dtype=jnp.int32)[:, None] * NXI
    xagg = (within + offsets).reshape(X).astype(jnp.int32)
    onehot = (xagg[None, :] == jnp.arange(NXI * N_GRP, dtype=jnp.int32)[:, None]).astype(jnp.float32)
    column_pad = jnp.pad(xagg, 1, constant_values=-1)
    same_xm = (column_pad[:-2] == xagg).astype(jnp.float32)[None, :, None, None]
    same_xp = (column_pad[2:] == xagg).astype(jnp.float32)[None, :, None, None]
    layer_pad = jnp.pad(zagg, 1, constant_values=-1)
    padded = jnp.pad(prolong, ((1, 1), (1, 1), (1, 1), (0, 0), (0, 0)))

    def one_layer(running, layer):
        coupling = lax.dynamic_index_in_dim(a_blocks, layer, 0, keepdims=False).astype(jnp.float32)
        window = lax.dynamic_slice_in_dim(padded, layer, 3, 0).astype(jnp.float32)
        centre = window[1, 1:-1, 1:-1]
        beside = [centre, window[1, 1:-1, :-2], window[1, 1:-1, 2:], window[1, :-2, 1:-1],
                  window[1, 2:, 1:-1], window[0, 1:-1, 1:-1], window[2, 1:-1, 1:-1]]
        products = [jnp.einsum('yxrs,yxsc->yxrc', coupling[..., k * B:(k + 1) * B], beside[k])
                    for k in range(7)]
        interval = layer_pad[layer + 1]
        same_zm = (layer_pad[layer] == interval).astype(jnp.float32)
        same_zp = (layer_pad[layer + 2] == interval).astype(jnp.float32)
        self_sum = (products[0] + products[3] + products[4] + same_xm * products[1]
                    + same_xp * products[2] + same_zm * products[5] + same_zp * products[6])
        slots = [self_sum, (1.0 - same_xm) * products[1], (1.0 - same_xp) * products[2],
                 (1.0 - same_zm) * products[5], (1.0 - same_zp) * products[6]]
        routed = jnp.concatenate(slots, axis=-1).astype(jnp.bfloat16).astype(jnp.float32)
        partial_sum = jnp.einsum('yxrc,yxrk->xck', centre, routed)
        coarse = jnp.einsum('ex,xck->eck', onehot, partial_sum, precision=lax.Precision.HIGHEST)
        current = lax.dynamic_index_in_dim(running, interval, 0, keepdims=True)
        running = lax.dynamic_update_index_in_dim(running, current + coarse[None], interval, 0)
        return running, None

    start = jnp.zeros((Z // 2, NXI * N_GRP, BC, 5 * BC), jnp.float32)
    running, _ = lax.scan(one_layer, start, jnp.arange(Z, dtype=jnp.int32))
    return running.astype(jnp.bfloat16)
```

```python
import functools
import jax
import jax.numpy as jnp
from jax import lax
from jax.experimental import pallas as pl
from jax.experimental.pallas import tpu as pltpu
from jax.sharding import PartitionSpec as P

F32, BF16 = jnp.float32, jnp.bfloat16
LANES = 128
CHUNKS = 2
STEP = 4
LIMIT = 36 << 20


def vmem_block(shape, index):
    return pl.BlockSpec(shape, lambda *grid: index)


def scalars():
    return pl.BlockSpec(memory_space=pltpu.SMEM)


def shifted(block, axis, distance):
    devices = range(lax.axis_size(axis))
    route = [(i, i + distance) for i in devices if i + distance in devices]
    return lax.ppermute(block, axis, route)


def matmul(left, right):
    return jnp.dot(left, right, preferred_element_type=F32)


def transposed_matmul(left, right):
    return lax.dot_general(left, right, (((0,), (0,)), ((), ())), preferred_element_type=F32)


def interval_of(xlen_ref, group, column):
    end, found = 0, 0
    for i in range(xlen_ref.shape[1]):
        end = end + xlen_ref[group, i]
        found = found + jnp.where(column >= end, 1, 0)
    return found


def aligned(low, high, end):
    return low // LANES * LANES, min(-(-high // LANES) * LANES, end)


def factor(flag, shape):
    return jnp.full(shape, jnp.where(flag, 1.0, 0.0), F32).astype(BF16)


def diagonal(blocks, low, first, high):
    rows, columns = blocks[0].shape
    parts = []
    if first > low:
        parts.append(jnp.zeros((first - low, columns * len(blocks)), BF16))
    none = jnp.zeros((rows, columns), BF16)
    for i, block in enumerate(blocks):
        parts.append(jnp.concatenate([block if i == j else none for j in range(len(blocks))], axis=1))
    end = first + rows * len(blocks)
    if high > end:
        parts.append(jnp.zeros((high - end, columns * len(blocks)), BF16))
    return jnp.concatenate(parts, axis=0)


def pack_kernel(a_ref, top_ref, left_ref, right_ref, *outs):
    messages, (left_out, right_out) = outs[:-2], outs[-2:]
    depth, columns, block = top_ref.shape[1:4]
    each = columns // len(messages)
    for c, out in enumerate(messages):

        def body(i, _, c=c, out=out):
            at = c * each + 2 * i
            out[:, pl.ds(2 * i, 2)] = top_ref[0, :, pl.ds(at, 2)]
            for y in range(depth):
                pair = [a_ref[0, y, at + j, :, :block] for j in range(2)]
                out[y, each + i] = jnp.concatenate(pair, axis=-1)
            return 0

        lax.fori_loop(0, each // 2, body, 0)
    left_out[...] = left_ref[:, :, 0]
    right_out[...] = right_ref[:, :, 0]


def pack(a_blocks, prolong):
    layers, depth, columns, block, coarse = prolong.shape
    each = columns // CHUNKS
    low, _ = aligned(6 * block, 7 * block, 7 * block)
    message = jax.ShapeDtypeStruct((depth, each + each // 2, block, coarse), BF16)
    edge = jax.ShapeDtypeStruct((layers, depth, block, coarse), BF16)
    return pl.pallas_call(
        pack_kernel,
        grid=(1,),
        in_specs=[
            vmem_block((1, depth, columns, block, LANES), (layers - 1, 0, 0, 0, low // LANES)),
            vmem_block((1, depth, columns, block, coarse), (layers - 1, 0, 0, 0, 0)),
            vmem_block((layers, depth, 1, block, coarse), (0, 0, 0, 0, 0)),
            vmem_block((layers, depth, 1, block, coarse), (0, 0, columns - 1, 0, 0)),
        ],
        out_specs=[vmem_block(message.shape, (0,) * 4)] * CHUNKS + [vmem_block(edge.shape, (0,) * 4)] * 2,
        out_shape=[message] * CHUNKS + [edge] * 2,
        compiler_params=pltpu.CompilerParams(vmem_limit_bytes=LIMIT),
        name="pack",
    )(a_blocks, prolong, prolong, prolong)


def main_kernel(halves, zagg_ref, xlen_ref, a_ref, p_ref, left_ref, right_ref, sums_ref, early_ref):
    layers, depth, columns, block, coarse = p_ref.shape
    wide = a_ref.shape[-1]
    step = a_ref.shape[2]
    shape = (block, coarse)
    dom, grp = lax.axis_index("dom"), lax.axis_index("grp")
    layer = pl.program_id(0)

    @pl.when((pl.program_id(0) == 0) & (pl.program_id(1) == 0))
    def _():
        def clear(i, _):
            for target in range(sums_ref.shape[0]):
                sums_ref[target, i] = jnp.zeros(sums_ref.shape[2:], F32)
            return 0

        lax.fori_loop(0, sums_ref.shape[1], clear, 0)

    at = dom * layers + layer
    mine = zagg_ref[at]
    target = mine - dom * halves + 1
    has_zm, has_zp = layer > 0, layer < layers - 1
    below = jnp.where(has_zm, layer - 1, 0)
    above = jnp.where(has_zp, layer + 1, layer)
    same_zm = has_zm & (zagg_ref[jnp.where(has_zm, at - 1, at)] == mine)
    same_zp = has_zp & (zagg_ref[jnp.where(has_zp, at + 1, at)] == mine)
    apart_zm = has_zm & jnp.logical_not(same_zm)
    apart_zp = has_zp & jnp.logical_not(same_zp)
    none = jnp.zeros(shape, BF16)

    def beside(x):
        has_xm, has_xp = x > 0, x < columns - 1
        before, after = jnp.where(has_xm, x - 1, 0), jnp.where(has_xp, x + 1, x)
        interval = interval_of(xlen_ref, grp, x)
        same_xm = has_xm & (interval_of(xlen_ref, grp, before) == interval)
        same_xp = has_xp & (interval_of(xlen_ref, grp, after) == interval)
        return interval, has_xm, has_xp, before, after, same_xm, same_xp

    def own(x):
        return p_ref[layer, :, x].reshape(depth * block, coarse)

    def pair(q, _):
        first = pl.program_id(1) * step + 2 * q
        info = [beside(first + j) for j in range(2)]
        zm_factor, zp_factor = factor(same_zm, shape), factor(same_zp, shape)
        factors = [(factor(i[5], shape), factor(i[6], shape)) for i in info]
        rows = [[], []]
        for y in range(depth):
            stacks = []
            for j in range(2):
                x, (_, _, _, before, after, _, _) = first + j, info[j]
                stacks.append(
                    jnp.concatenate(
                        [
                            p_ref[layer, y, x],
                            p_ref[layer, y, before] * factors[j][0],
                            p_ref[layer, y, after] * factors[j][1],
                            p_ref[layer, y - 1, x] if y > 0 else none,
                            p_ref[layer, y + 1, x] if y < depth - 1 else none,
                            p_ref[below, y, x] * zm_factor,
                            p_ref[above, y, x] * zp_factor,
                        ],
                        axis=0,
                    )
                )
            left = a_ref[0, y, pl.ds(2 * q, 2)].reshape(2 * block, wide)
            both = matmul(left, jnp.concatenate(stacks, axis=1))
            for j in range(2):
                rows[j].append(
                    both[j * block : (j + 1) * block, j * coarse : (j + 1) * coarse].astype(BF16)
                )
        for j in range(2):
            sums_ref[target, info[j][0], :, :coarse] += transposed_matmul(
                own(first + j), jnp.concatenate(rows[j], axis=0)
            )
        return 0

    lax.fori_loop(0, step // 2, pair, 0)

    def split(i, x, interval, slot, k, blocks):
        low, high = aligned(k * block, (k + 2) * block, wide)
        rows = []
        for y in range(depth):
            right = diagonal(blocks(y), low, k * block, high)
            rows.append(matmul(a_ref[0, y, i, :, low:high], right).astype(BF16))
        lanes = slice(slot * coarse, (slot + 2) * coarse)
        sums_ref[target, interval, :, lanes] += transposed_matmul(own(x), jnp.concatenate(rows, axis=0))

    def along_x(i, _):
        x = pl.program_id(1) * step + i
        interval, has_xm, has_xp, before, after, same_xm, same_xp = beside(x)

        @pl.when(jnp.logical_not(same_xm & same_xp))
        def _():
            inner_xm = factor(has_xm & jnp.logical_not(same_xm), shape)
            inner_xp = factor(has_xp & jnp.logical_not(same_xp), shape)
            outer_xm, outer_xp = factor(jnp.logical_not(has_xm), shape), factor(jnp.logical_not(has_xp), shape)
            split(
                i,
                x,
                interval,
                1,
                1,
                lambda y: [
                    p_ref[layer, y, before] * inner_xm + left_ref[layer, y] * outer_xm,
                    p_ref[layer, y, after] * inner_xp + right_ref[layer, y] * outer_xp,
                ],
            )

        return 0

    lax.fori_loop(0, step, along_x, 0)

    @pl.when(apart_zm | apart_zp)
    def _():
        zm_factor, zp_factor = factor(apart_zm, shape), factor(apart_zp, shape)

        def along_z(i, _):
            x = pl.program_id(1) * step + i
            split(
                i,
                x,
                interval_of(xlen_ref, grp, x),
                3,
                5,
                lambda y: [p_ref[below, y, x] * zm_factor, p_ref[above, y, x] * zp_factor],
            )
            return 0

        lax.fori_loop(0, step, along_z, 0)

    @pl.when((layer == layers - 1) & (pl.program_id(1) == pl.num_programs(1) - 1))
    def _():
        def emit(i, _):
            early_ref[i, :, : 2 * coarse] = sums_ref[0, i, :, coarse : 3 * coarse].astype(BF16)
            early_ref[i, :, 2 * coarse :] = sums_ref[0, i, :, 4 * coarse :].astype(BF16)
            return 0

        lax.fori_loop(0, early_ref.shape[0], emit, 0)


def main(halves, zagg, xlen, a_blocks, prolong, left, right):
    layers, depth, columns, block, coarse = prolong.shape
    intervals = xlen.shape[1]
    sums = jax.ShapeDtypeStruct((halves + 1, intervals, coarse, 5 * coarse), F32)
    early = jax.ShapeDtypeStruct((intervals, coarse, 3 * coarse), BF16)
    step = STEP if columns % STEP == 0 else 2

    def whole(shape):
        return pl.BlockSpec(shape, lambda *grid: (0,) * len(shape), pipeline_mode=pl.Buffered(1))

    flops = layers * columns * depth * 2 * block * coarse * 12 * block
    return pl.pallas_call(
        functools.partial(main_kernel, halves),
        grid=(layers, columns // step),
        in_specs=[
            scalars(),
            scalars(),
            pl.BlockSpec((1, depth, step, block, a_blocks.shape[-1]), lambda i, j: (i, 0, j, 0, 0)),
            whole(prolong.shape),
            whole(left.shape),
            whole(right.shape),
        ],
        out_specs=[vmem_block(sums.shape, (0,) * 4), vmem_block(early.shape, (0,) * 3)],
        out_shape=[sums, early],
        cost_estimate=pl.CostEstimate(flops=flops * 4, bytes_accessed=40 << 20, transcendentals=0),
        compiler_params=pltpu.CompilerParams(vmem_limit_bytes=LIMIT),
        name="coarsen",
    )(zagg, xlen, a_blocks, prolong, left, right)


def boundary_kernel(chunk, last, zagg_ref, xlen_ref, message_ref, a_ref, p_ref, carried_ref, *rest):
    if chunk > 0:
        base_ref, rest = rest[0], rest[1:]
    depth, _, block, coarse = message_ref.shape
    each = p_ref.shape[2]
    dom, grp = lax.axis_index("dom"), lax.axis_index("grp")
    sums_ref = rest[-1]
    sums_ref[...] = base_ref[...] if chunk > 0 else jnp.zeros_like(sums_ref)
    low, high = aligned(5 * block, 6 * block, 7 * block)

    def interval(q, j):
        return interval_of(xlen_ref, grp, chunk * each + 2 * q + j)

    def upper(q, _):
        rows = [[], []]
        for y in range(depth):
            mine = [p_ref[0, y, 2 * q + j] for j in range(2)]
            both = matmul(message_ref[y, each + q], diagonal(mine, 0, 0, 2 * block))
            for j in range(2):
                rows[j].append(both[:, j * coarse : (j + 1) * coarse].astype(BF16))
        for j in range(2):
            theirs = message_ref[:, 2 * q + j].reshape(depth * block, coarse)
            sums_ref[0, interval(q, j)] += transposed_matmul(theirs, jnp.concatenate(rows[j], axis=0))
        return 0

    def lower(q, _):
        rows = [[], []]
        for y in range(depth):
            theirs = jnp.concatenate([message_ref[y, 2 * q + j] for j in range(2)], axis=1)
            left = a_ref[0, y, pl.ds(2 * q, 2)].reshape(2 * block, high - low)
            both = matmul(left, diagonal([theirs], low, 5 * block, high))
            for j in range(2):
                rows[j].append(both[j * block : (j + 1) * block, j * coarse : (j + 1) * coarse].astype(BF16))
        for j in range(2):
            own = p_ref[0, :, 2 * q + j].reshape(depth * block, coarse)
            sums_ref[1, interval(q, j)] += transposed_matmul(own, jnp.concatenate(rows[j], axis=0))
        return 0

    lax.fori_loop(0, each // 2, upper, 0)
    lax.fori_loop(0, each // 2, lower, 0)
    if last:
        late_ref, owned_ref = rest[:2]
        layers = zagg_ref.shape[0] // lax.axis_size("dom")
        at = dom * layers
        same = (at > 0) & (zagg_ref[jnp.where(at > 0, at - 1, 0)] == zagg_ref[at])
        joined = jnp.where(same, 1.0, 0.0)
        late_ref[...] = (carried_ref[0] + sums_ref[0] + joined * sums_ref[1]).astype(BF16)
        owned_ref[...] = (1.0 - joined) * sums_ref[1]


def boundary(chunk, zagg, xlen, message, a_blocks, prolong, carried, base=None):
    layers, depth, columns, block, coarse = prolong.shape
    intervals = xlen.shape[1]
    each = columns // CHUNKS
    last = chunk == CHUNKS - 1
    low, high = aligned(5 * block, 6 * block, 7 * block)
    sums = jax.ShapeDtypeStruct((2, intervals, coarse, coarse), F32)
    in_specs = [
        scalars(),
        scalars(),
        vmem_block(message.shape, (0,) * 4),
        vmem_block((1, depth, each, block, high - low), (0, 0, chunk, 0, low // LANES)),
        vmem_block((1, depth, each, block, coarse), (0, 0, chunk, 0, 0)),
        vmem_block((1, intervals, coarse, coarse), (0,) * 4),
    ]
    operands = [zagg, xlen, message, a_blocks, prolong, carried]
    if base is not None:
        in_specs.append(vmem_block(sums.shape, (0,) * 4))
        operands.append(base)
    out_specs, out_shape, scratch = [vmem_block(sums.shape, (0,) * 4)], [sums], []
    if last:
        late = jax.ShapeDtypeStruct((intervals, coarse, coarse), BF16)
        owned = jax.ShapeDtypeStruct((intervals, coarse, coarse), F32)
        out_specs, out_shape = [vmem_block(late.shape, (0,) * 3)] * 2, [late, owned]
        scratch = [pltpu.VMEM(sums.shape, F32)]
    return pl.pallas_call(
        functools.partial(boundary_kernel, chunk, last),
        grid=(1,),
        in_specs=in_specs,
        out_specs=out_specs,
        out_shape=out_shape,
        scratch_shapes=scratch,
        compiler_params=pltpu.CompilerParams(vmem_limit_bytes=LIMIT),
        name="boundary_" + str(chunk),
    )(*operands)


def final_kernel(zagg_ref, sums_ref, owned_ref, early_ref, late_ref, out_ref):
    coarse = sums_ref.shape[2]
    dom = lax.axis_index("dom")
    layers = zagg_ref.shape[0] // lax.axis_size("dom")
    half, halves = pl.program_id(0), pl.num_programs(0)
    first = jnp.where(half == 0, 1.0, 0.0)
    last = jnp.where(half == halves - 1, 1.0, 0.0)
    end = (dom + 1) * layers
    following = jnp.where(end < zagg_ref.shape[0], end, end - 1)
    joined = jnp.where(zagg_ref[following] == zagg_ref[end - 1], last, 0.0)

    def lanes(slot):
        return slice(slot * coarse, (slot + 1) * coarse)

    late = late_ref[...].astype(F32)

    def early(index):
        return last * early_ref[:, :, lanes(index)].astype(F32)

    out_ref[0, :, :, lanes(0)] = (sums_ref[0, :, :, lanes(0)] + joined * late).astype(BF16)
    out_ref[0, :, :, lanes(1)] = (sums_ref[0, :, :, lanes(1)] + early(0)).astype(BF16)
    out_ref[0, :, :, lanes(2)] = (sums_ref[0, :, :, lanes(2)] + early(1)).astype(BF16)
    out_ref[0, :, :, lanes(3)] = (sums_ref[0, :, :, lanes(3)] + first * owned_ref[...]).astype(BF16)
    out_ref[0, :, :, lanes(4)] = (
        sums_ref[0, :, :, lanes(4)] + early(2) + (last - joined) * late
    ).astype(BF16)


def final(halves, zagg, sums, owned, early, late):
    _, intervals, coarse, wide = sums.shape
    return pl.pallas_call(
        final_kernel,
        grid=(halves,),
        in_specs=[
            scalars(),
            pl.BlockSpec((1, intervals, coarse, wide), lambda h: (h + 1, 0, 0, 0)),
            vmem_block(owned.shape, (0,) * 3),
            vmem_block(early.shape, (0,) * 3),
            vmem_block(late.shape, (0,) * 3),
        ],
        out_specs=pl.BlockSpec((1, intervals, coarse, wide), lambda h: (h, 0, 0, 0)),
        out_shape=jax.ShapeDtypeStruct((halves, intervals, coarse, wide), BF16),
        name="finish",
    )(zagg, sums, owned, early, late)


def in_hbm(block):
    return pltpu.with_memory_space_constraint(block, pltpu.HBM)


def per_device(a_blocks, prolong, zagg, xlen):
    halves = prolong.shape[0] // 2
    *messages, left_edge, right_edge = pack(a_blocks, prolong)
    arrived = [in_hbm(shifted(message, "dom", 1)) for message in messages]
    left = in_hbm(shifted(right_edge, "grp", 1))
    right = in_hbm(shifted(left_edge, "grp", -1))
    sums, early = main(halves, zagg, xlen, a_blocks, prolong, left, right)
    early = in_hbm(shifted(early, "dom", -1))
    beyond = None
    for chunk, message in enumerate(arrived):
        outs = boundary(chunk, zagg, xlen, message, a_blocks, prolong, sums, beyond)
        beyond = outs[0]
    late, owned = outs
    late = in_hbm(shifted(late, "dom", -1))
    return final(halves, zagg, sums, owned, early, late)


def solution(mesh):
    in_specs = (P("dom", None, "grp", None, None), P("dom", None, "grp", None, None), P(), P())
    out_specs = P("dom", "grp", None, None)
    return jax.shard_map(per_device, mesh=mesh, in_specs=in_specs, out_specs=out_specs, check_vma=False)
```

```python
import functools
import jax
import jax.numpy as jnp
from jax import lax
from jax.experimental import pallas as pl
from jax.experimental.pallas import tpu as pltpu
from jax.sharding import PartitionSpec as P


F32, BF16 = jnp.float32, jnp.bfloat16
LANES = 128
CHUNKS = 2
LIMIT = 36 << 20


def vmem_block(shape, index):
    return pl.BlockSpec(shape, lambda *grid: index)


def scalars():
    return pl.BlockSpec(memory_space=pltpu.SMEM)


def in_vmem():
    return pl.BlockSpec(memory_space=pltpu.VMEM)


def shifted(block, axis, distance):
    devices = range(lax.axis_size(axis))
    route = [(i, i + distance) for i in devices if i + distance in devices]
    return lax.ppermute(block, axis, route)


def matmul(left, right):
    return jnp.dot(left, right, preferred_element_type=F32)


def transposed_matmul(left, right):
    return lax.dot_general(left, right, (((0,), (0,)), ((), ())), preferred_element_type=F32)


def interval_of(xlen_ref, group, column):
    end, found = 0, 0
    for i in range(xlen_ref.shape[1]):
        end = end + xlen_ref[group, i]
        found = found + jnp.where(column >= end, 1, 0)
    return found


def aligned(low, high, end):
    return low // LANES * LANES, min(-(-high // LANES) * LANES, end)


def factor(flag, shape):
    return jnp.full(shape, jnp.where(flag, 1.0, 0.0), F32).astype(BF16)


def diagonal(blocks, low, first, high):
    rows, columns = blocks[0].shape
    parts = []
    if first > low:
        parts.append(jnp.zeros((first - low, columns * len(blocks)), BF16))
    none = jnp.zeros((rows, columns), BF16)
    for i, block in enumerate(blocks):
        parts.append(jnp.concatenate([block if i == j else none for j in range(len(blocks))], axis=1))
    end = first + rows * len(blocks)
    if high > end:
        parts.append(jnp.zeros((high - end, columns * len(blocks)), BF16))
    return jnp.concatenate(parts, axis=0)


def pack_kernel(a_ref, top_ref, left_ref, right_ref, *outs):
    messages, (left_out, right_out) = outs[:-2], outs[-2:]
    depth, columns, block = top_ref.shape[1:4]
    each = columns // len(messages)
    for c, out in enumerate(messages):

        def body(i, _, c=c, out=out):
            at = c * each + 2 * i
            out[:, pl.ds(2 * i, 2)] = top_ref[0, :, pl.ds(at, 2)]
            for y in range(depth):
                pair = [a_ref[0, y, at + j, :, :block] for j in range(2)]
                out[y, each + i] = jnp.concatenate(pair, axis=-1)
            return 0

        lax.fori_loop(0, each // 2, body, 0)
    left_out[...] = left_ref[:, :, 0]
    right_out[...] = right_ref[:, :, 0]


def pack(a_blocks, prolong):
    layers, depth, columns, block, coarse = prolong.shape
    each = columns // CHUNKS
    low, _ = aligned(6 * block, 7 * block, 7 * block)
    message = jax.ShapeDtypeStruct((depth, each + each // 2, block, coarse), BF16)
    edge = jax.ShapeDtypeStruct((layers, depth, block, coarse), BF16)
    return pl.pallas_call(
        pack_kernel,
        grid=(1,),
        in_specs=[
            vmem_block((1, depth, columns, block, LANES), (layers - 1, 0, 0, 0, low // LANES)),
            vmem_block((1, depth, columns, block, coarse), (layers - 1, 0, 0, 0, 0)),
            vmem_block((layers, depth, 1, block, coarse), (0, 0, 0, 0, 0)),
            vmem_block((layers, depth, 1, block, coarse), (0, 0, columns - 1, 0, 0)),
        ],
        out_specs=[vmem_block(message.shape, (0,) * 4)] * CHUNKS + [vmem_block(edge.shape, (0,) * 4)] * 2,
        out_shape=[message] * CHUNKS + [edge] * 2,
        compiler_params=pltpu.CompilerParams(vmem_limit_bytes=LIMIT),
        name="pack",
    )(a_blocks, prolong, prolong, prolong)


def main_kernel(halves, zagg_ref, xlen_ref, a_ref, p_ref, left_ref, right_ref, sums_ref, early_ref, rows_ref):
    layers, depth, columns, block, coarse = p_ref.shape
    intervals = sums_ref.shape[1]
    wide = a_ref.shape[-1]
    shape = (block, coarse)
    dom, grp = lax.axis_index("dom"), lax.axis_index("grp")
    layer = pl.program_id(0)

    @pl.when(layer == 0)
    def _():
        def clear(i, _):
            for target in range(sums_ref.shape[0]):
                sums_ref[target, i] = jnp.zeros(sums_ref.shape[2:], F32)
            return 0

        lax.fori_loop(0, intervals, clear, 0)

    rows_ref[...] = jnp.zeros_like(rows_ref)

    at = dom * layers + layer
    mine = zagg_ref[at]
    target = mine - dom * halves + 1
    has_zm, has_zp = layer > 0, layer < layers - 1
    below = jnp.where(has_zm, layer - 1, 0)
    above = jnp.where(has_zp, layer + 1, layer)
    same_zm = has_zm & (zagg_ref[jnp.where(has_zm, at - 1, at)] == mine)
    same_zp = has_zp & (zagg_ref[jnp.where(has_zp, at + 1, at)] == mine)
    none = jnp.zeros(shape, BF16)

    def settle(pending):
        for j in range(2):
            x, interval, slot = pending[j]
            own = p_ref[layer, :, x].reshape(depth * block, coarse)
            sums_ref[target, interval, slot] += transposed_matmul(own, rows_ref[j])

    def keep(products):
        for y, both in enumerate(products):
            for j in range(2):
                part = both[j * block : (j + 1) * block, j * coarse : (j + 1) * coarse]
                rows_ref[j, y * block : (y + 1) * block] = part.astype(BF16)

    def inner(q, pending):
        settle(pending)
        zm_factor, zp_factor = factor(same_zm, shape), factor(same_zp, shape)
        info = []
        for j in range(2):
            x = 2 * q + j
            has_xm, has_xp = x > 0, x < columns - 1
            before, after = jnp.where(has_xm, x - 1, 0), jnp.where(has_xp, x + 1, x)
            interval = interval_of(xlen_ref, grp, x)
            same_xm = has_xm & (interval_of(xlen_ref, grp, before) == interval)
            same_xp = has_xp & (interval_of(xlen_ref, grp, after) == interval)
            info.append((x, interval, before, after, factor(same_xm, shape), factor(same_xp, shape)))
        products = []
        for y in range(depth):
            stacks = []
            for x, _, before, after, xm_factor, xp_factor in info:
                stacks.append(
                    jnp.concatenate(
                        [
                            p_ref[layer, y, x],
                            p_ref[layer, y, before] * xm_factor,
                            p_ref[layer, y, after] * xp_factor,
                            p_ref[layer, y - 1, x] if y > 0 else none,
                            p_ref[layer, y + 1, x] if y < depth - 1 else none,
                            p_ref[below, y, x] * zm_factor,
                            p_ref[above, y, x] * zp_factor,
                        ],
                        axis=0,
                    )
                )
            left = a_ref[0, y, pl.ds(2 * q, 2)].reshape(2 * block, wide)
            products.append(matmul(left, jnp.concatenate(stacks, axis=1)))
        keep(products)
        return tuple((i[0], i[1], jnp.int32(0)) for i in info)

    def across_x(i, pending):
        settle(pending)
        low, high = aligned(block, 3 * block, wide)
        end = 0
        for n in range(intervals):
            end = end + jnp.where(n <= i, xlen_ref[grp, n], 0)
        inside = end < columns
        x0, x1 = end - 1, jnp.where(inside, end, 0)
        within, beyond = factor(inside, shape), factor(jnp.logical_not(inside), shape)
        products = []
        for y in range(depth):
            before = p_ref[layer, y, x0] * within + left_ref[layer, y] * beyond
            after = p_ref[layer, y, x1] * within + right_ref[layer, y] * beyond
            stack = jnp.concatenate(
                [
                    jnp.zeros((block - low, 2 * coarse), BF16),
                    jnp.concatenate([none, before], axis=1),
                    jnp.concatenate([after, none], axis=1),
                    jnp.zeros((high - 3 * block, 2 * coarse), BF16),
                ],
                axis=0,
            )
            left = jnp.concatenate([a_ref[0, y, x0, :, low:high], a_ref[0, y, x1, :, low:high]], axis=0)
            products.append(matmul(left, stack))
        keep(products)
        return ((x0, i, jnp.int32(2)), (x1, jnp.where(i < intervals - 1, i + 1, 0), jnp.int32(1)))

    def across_z(k, slot, other):
        low, high = aligned(k * block, (k + 1) * block, wide)

        def body(q, pending):
            settle(pending)
            products = []
            for y in range(depth):
                beside = jnp.concatenate([p_ref[other, y, 2 * q + j] for j in range(2)], axis=1)
                left = a_ref[0, y, pl.ds(2 * q, 2), :, low:high].reshape(2 * block, high - low)
                products.append(matmul(left, diagonal([beside], low, k * block, high)))
            keep(products)
            return tuple((2 * q + j, interval_of(xlen_ref, grp, 2 * q + j), jnp.int32(slot)) for j in range(2))

        return body

    zero = jnp.int32(0)
    pending = ((zero, zero, zero), (zero, zero, zero))
    pairs = columns // 2
    pending = lax.fori_loop(0, pairs, inner, pending)
    pending = lax.fori_loop(0, intervals, across_x, pending)
    pairs_zm = jnp.where(has_zm & jnp.logical_not(same_zm), pairs, 0)
    pairs_zp = jnp.where(has_zp & jnp.logical_not(same_zp), pairs, 0)
    pending = lax.fori_loop(0, pairs_zm, across_z(5, 3, below), pending)
    pending = lax.fori_loop(0, pairs_zp, across_z(6, 4, above), pending)
    settle(pending)

    @pl.when(layer == layers - 1)
    def _():
        def emit(i, _):
            for n, slot in enumerate((1, 2, 4)):
                early_ref[n, i] = sums_ref[0, i, slot].astype(BF16)
            return 0

        lax.fori_loop(0, intervals, emit, 0)


def main(halves, zagg, xlen, a_blocks, prolong, left, right):
    layers, depth, columns, block, coarse = prolong.shape
    intervals = xlen.shape[1]
    sums = jax.ShapeDtypeStruct((halves + 1, intervals, 5, coarse, coarse), F32)
    early = jax.ShapeDtypeStruct((3, intervals, coarse, coarse), BF16)

    def whole(shape):
        return pl.BlockSpec(shape, lambda *grid: (0,) * len(shape), pipeline_mode=pl.Buffered(1))

    flops = layers * columns * depth * 2 * block * coarse * 12 * block
    return pl.pallas_call(
        functools.partial(main_kernel, halves),
        grid=(layers,),
        in_specs=[
            scalars(),
            scalars(),
            pl.BlockSpec((1, depth, columns, block, a_blocks.shape[-1]), lambda i: (i, 0, 0, 0, 0)),
            whole(prolong.shape),
            in_vmem(),
            in_vmem(),
        ],
        out_specs=[vmem_block(sums.shape, (0,) * 5), vmem_block(early.shape, (0,) * 4)],
        out_shape=[sums, early],
        scratch_shapes=[pltpu.VMEM((2, depth * block, coarse), BF16)],
        cost_estimate=pl.CostEstimate(flops=flops * 4, bytes_accessed=40 << 20, transcendentals=0),
        compiler_params=pltpu.CompilerParams(vmem_limit_bytes=LIMIT),
        name="coarsen",
    )(zagg, xlen, a_blocks, prolong, left, right)


def boundary_kernel(chunk, last, zagg_ref, xlen_ref, message_ref, a_ref, p_ref, carried_ref, *rest):
    if chunk > 0:
        base_ref, rest = rest[0], rest[1:]
    depth, _, block, coarse = message_ref.shape
    each = p_ref.shape[2]
    dom, grp = lax.axis_index("dom"), lax.axis_index("grp")
    sums_ref = rest[-1]
    sums_ref[...] = base_ref[...] if chunk > 0 else jnp.zeros_like(sums_ref)
    low, high = aligned(5 * block, 6 * block, 7 * block)

    def interval(q, j):
        return interval_of(xlen_ref, grp, chunk * each + 2 * q + j)

    def upper(q, _):
        rows = [[], []]
        for y in range(depth):
            mine = [p_ref[0, y, 2 * q + j] for j in range(2)]
            both = matmul(message_ref[y, each + q], diagonal(mine, 0, 0, 2 * block))
            for j in range(2):
                rows[j].append(both[:, j * coarse : (j + 1) * coarse].astype(BF16))
        for j in range(2):
            theirs = message_ref[:, 2 * q + j].reshape(depth * block, coarse)
            sums_ref[0, interval(q, j)] += transposed_matmul(theirs, jnp.concatenate(rows[j], axis=0))
        return 0

    def lower(q, _):
        rows = [[], []]
        for y in range(depth):
            theirs = jnp.concatenate([message_ref[y, 2 * q + j] for j in range(2)], axis=1)
            left = a_ref[0, y, pl.ds(2 * q, 2)].reshape(2 * block, high - low)
            both = matmul(left, diagonal([theirs], low, 5 * block, high))
            for j in range(2):
                rows[j].append(both[j * block : (j + 1) * block, j * coarse : (j + 1) * coarse].astype(BF16))
        for j in range(2):
            own = p_ref[0, :, 2 * q + j].reshape(depth * block, coarse)
            sums_ref[1, interval(q, j)] += transposed_matmul(own, jnp.concatenate(rows[j], axis=0))
        return 0

    lax.fori_loop(0, each // 2, upper, 0)
    lax.fori_loop(0, each // 2, lower, 0)
    if last:
        late_ref, owned_ref = rest[:2]
        layers = zagg_ref.shape[0] // lax.axis_size("dom")
        at = dom * layers
        same = (at > 0) & (zagg_ref[jnp.where(at > 0, at - 1, 0)] == zagg_ref[at])
        joined = jnp.where(same, 1.0, 0.0)
        late_ref[...] = (carried_ref[0, :, 0] + sums_ref[0] + joined * sums_ref[1]).astype(BF16)
        owned_ref[...] = (1.0 - joined) * sums_ref[1]


def boundary(chunk, zagg, xlen, message, a_blocks, prolong, carried, base=None):
    _, depth, columns, block, coarse = prolong.shape
    intervals = xlen.shape[1]
    each = columns // CHUNKS
    last = chunk == CHUNKS - 1
    low, high = aligned(5 * block, 6 * block, 7 * block)
    sums = jax.ShapeDtypeStruct((2, intervals, coarse, coarse), F32)
    in_specs = [
        scalars(),
        scalars(),
        in_vmem(),
        vmem_block((1, depth, each, block, high - low), (0, 0, chunk, 0, low // LANES)),
        vmem_block((1, depth, each, block, coarse), (0, 0, chunk, 0, 0)),
        vmem_block((1, intervals, 1, coarse, coarse), (0,) * 5),
    ]
    operands = [zagg, xlen, message, a_blocks, prolong, carried]
    if base is not None:
        in_specs.append(vmem_block(sums.shape, (0,) * 4))
        operands.append(base)
    out_specs, out_shape, scratch = [vmem_block(sums.shape, (0,) * 4)], [sums], []
    if last:
        late = jax.ShapeDtypeStruct((intervals, coarse, coarse), BF16)
        owned = jax.ShapeDtypeStruct((intervals, coarse, coarse), F32)
        out_specs, out_shape = [vmem_block(late.shape, (0,) * 3)] * 2, [late, owned]
        scratch = [pltpu.VMEM(sums.shape, F32)]
    return pl.pallas_call(
        functools.partial(boundary_kernel, chunk, last),
        grid=(1,),
        in_specs=in_specs,
        out_specs=out_specs,
        out_shape=out_shape,
        scratch_shapes=scratch,
        compiler_params=pltpu.CompilerParams(vmem_limit_bytes=LIMIT),
    )(*operands)


def final_kernel(zagg_ref, sums_ref, owned_ref, early_ref, late_ref, out_ref):
    coarse = sums_ref.shape[-1]
    dom = lax.axis_index("dom")
    layers = zagg_ref.shape[0] // lax.axis_size("dom")
    half, halves = pl.program_id(0), pl.num_programs(0)
    first = jnp.where(half == 0, 1.0, 0.0)
    last = jnp.where(half == halves - 1, 1.0, 0.0)
    end = (dom + 1) * layers
    following = jnp.where(end < zagg_ref.shape[0], end, end - 1)
    joined = jnp.where(zagg_ref[following] == zagg_ref[end - 1], last, 0.0)

    def put(slot, value):
        out_ref[0, :, :, slot * coarse : (slot + 1) * coarse] = value.astype(BF16)

    late = late_ref[...].astype(F32)

    def early(n):
        return last * early_ref[n].astype(F32)

    put(0, sums_ref[0, :, 0] + joined * late)
    put(1, sums_ref[0, :, 1] + early(0))
    put(2, sums_ref[0, :, 2] + early(1))
    put(3, sums_ref[0, :, 3] + first * owned_ref[...])
    put(4, sums_ref[0, :, 4] + early(2) + (last - joined) * late)


def final(halves, zagg, sums, owned, early, late):
    _, intervals, slots, coarse, _ = sums.shape
    return pl.pallas_call(
        final_kernel,
        grid=(halves,),
        in_specs=[
            scalars(),
            pl.BlockSpec((1, intervals, slots, coarse, coarse), lambda h: (h + 1, 0, 0, 0, 0)),
            vmem_block(owned.shape, (0,) * 3),
            in_vmem(),
            in_vmem(),
        ],
        out_specs=pl.BlockSpec((1, intervals, coarse, slots * coarse), lambda h: (h, 0, 0, 0)),
        out_shape=jax.ShapeDtypeStruct((halves, intervals, coarse, slots * coarse), BF16),
        compiler_params=pltpu.CompilerParams(vmem_limit_bytes=LIMIT),
        name="finish",
    )(zagg, sums, owned, early, late)


def per_device(a_blocks, prolong, zagg, xlen):
    halves = prolong.shape[0] // 2
    prolong = pltpu.with_memory_space_constraint(prolong, pltpu.HBM)
    *messages, left_edge, right_edge = pack(a_blocks, prolong)
    arrived = []
    for message in messages:
        arrived.append(shifted(message, "dom", 1))
    left = shifted(right_edge, "grp", 1)
    right = shifted(left_edge, "grp", -1)
    sums, early = main(halves, zagg, xlen, a_blocks, prolong, left, right)
    early = shifted(early, "dom", -1)
    beyond = None
    for chunk, message in enumerate(arrived):
        outs = boundary(chunk, zagg, xlen, message, a_blocks, prolong, sums, beyond)
        beyond = outs[0]
    late, owned = outs
    late = shifted(late, "dom", -1)
    return final(halves, zagg, sums, owned, early, late)


def solution(mesh):
    in_specs = (P("dom", None, "grp", None, None), P("dom", None, "grp", None, None), P(), P())
    out_specs = P("dom", "grp", None, None)
    return jax.shard_map(per_device, mesh=mesh, in_specs=in_specs, out_specs=out_specs, check_vma=False)
```

```python
import functools
import jax
import jax.numpy as jnp
from jax import lax
from jax.experimental import pallas as pl
from jax.experimental.pallas import tpu as pltpu
from jax.sharding import PartitionSpec as P


F32, BF16 = jnp.float32, jnp.bfloat16
LANES = 128
LIMIT = 36 << 20


def vmem_block(shape, index):
    return pl.BlockSpec(shape, lambda *grid: index)


def scalars():
    return pl.BlockSpec(memory_space=pltpu.SMEM)


def in_vmem():
    return pl.BlockSpec(memory_space=pltpu.VMEM)


def shifted(block, axis, distance):
    devices = range(lax.axis_size(axis))
    route = [(i, i + distance) for i in devices if i + distance in devices]
    return lax.ppermute(block, axis, route)


def matmul(left, right):
    return jnp.dot(left, right, preferred_element_type=F32)


def transposed_matmul(left, right):
    return lax.dot_general(left, right, (((0,), (0,)), ((), ())), preferred_element_type=F32)


def interval_of(xlen_ref, group, column):
    end, found = 0, 0
    for i in range(xlen_ref.shape[1]):
        end = end + xlen_ref[group, i]
        found = found + jnp.where(column >= end, 1, 0)
    return found


def aligned(low, high, end):
    return low // LANES * LANES, min(-(-high // LANES) * LANES, end)


def factor(flag, shape):
    return jnp.full(shape, jnp.where(flag, 1.0, 0.0), F32).astype(BF16)


def diagonal(blocks, low, first, high):
    rows, columns = blocks[0].shape
    parts = []
    if first > low:
        parts.append(jnp.zeros((first - low, columns * len(blocks)), BF16))
    none = jnp.zeros((rows, columns), BF16)
    for i, block in enumerate(blocks):
        parts.append(jnp.concatenate([block if i == j else none for j in range(len(blocks))], axis=1))
    end = first + rows * len(blocks)
    if high > end:
        parts.append(jnp.zeros((high - end, columns * len(blocks)), BF16))
    return jnp.concatenate(parts, axis=0)


def top_kernel(p_ref, out_ref, sem):
    copy = pltpu.make_async_copy(p_ref.at[p_ref.shape[0] - 1], out_ref, sem)
    copy.start()
    copy.wait()


def top(prolong):
    return pl.pallas_call(
        top_kernel,
        in_specs=[pl.BlockSpec(memory_space=pltpu.HBM)],
        out_specs=in_vmem(),
        out_shape=jax.ShapeDtypeStruct(prolong.shape[1:], BF16),
        scratch_shapes=[pltpu.SemaphoreType.DMA],
        compiler_params=pltpu.CompilerParams(vmem_limit_bytes=LIMIT),
        name="top",
    )(prolong)


def pack_kernel(a_ref, p_ref, after_ref, pairs_ref, left_ref, right_ref, sems):
    _, depth, block, _ = left_ref.shape
    copies = [
        pltpu.make_async_copy(p_ref.at[:, :, 0], left_ref, sems.at[0]),
        pltpu.make_async_copy(p_ref.at[:, :, p_ref.shape[2] - 1], right_ref, sems.at[1]),
    ]
    for copy in copies:
        copy.start()

    def body(i, _):
        for y in range(depth):
            pair = [a_ref[0, y, 2 * i + j, :, :block] for j in range(2)]
            pairs_ref[y, i] = jnp.concatenate(pair, axis=-1)
        return 0

    lax.fori_loop(0, pairs_ref.shape[1], body, 0)
    for copy in copies:
        copy.wait()


def pack(a_blocks, prolong, after):
    layers, depth, columns, block, coarse = prolong.shape
    low, _ = aligned(6 * block, 7 * block, 7 * block)
    pairs = jax.ShapeDtypeStruct((depth, columns // 2, block, 2 * block), BF16)
    edge = jax.ShapeDtypeStruct((layers, depth, block, coarse), BF16)
    return pl.pallas_call(
        pack_kernel,
        grid=(1,),
        in_specs=[
            vmem_block((1, depth, columns, block, LANES), (layers - 1, 0, 0, 0, low // LANES)),
            pl.BlockSpec(memory_space=pltpu.HBM),
            pl.BlockSpec(memory_space=pl.ANY),
        ],
        out_specs=[in_vmem()] * 3,
        out_shape=[pairs, edge, edge],
        scratch_shapes=[pltpu.SemaphoreType.DMA((2,))],
        compiler_params=pltpu.CompilerParams(vmem_limit_bytes=LIMIT),
        name="pack",
    )(a_blocks, prolong, after)


def main_kernel(halves, zagg_ref, xlen_ref, a_ref, p_ref, sums_ref, rows_ref):
    layers, depth, columns, block, coarse = p_ref.shape
    intervals = sums_ref.shape[1]
    wide = a_ref.shape[-1]
    shape = (block, coarse)
    dom, grp = lax.axis_index("dom"), lax.axis_index("grp")
    layer = pl.program_id(0)

    @pl.when(layer == 0)
    def _():
        def clear(i, _):
            for target in range(sums_ref.shape[0]):
                sums_ref[target, i] = jnp.zeros(sums_ref.shape[2:], F32)
            return 0

        lax.fori_loop(0, intervals, clear, 0)

    rows_ref[...] = jnp.zeros_like(rows_ref)

    at = dom * layers + layer
    mine = zagg_ref[at]
    target = mine - dom * halves + 1
    has_zm, has_zp = layer > 0, layer < layers - 1
    below = jnp.where(has_zm, layer - 1, 0)
    above = jnp.where(has_zp, layer + 1, layer)
    same_zm = has_zm & (zagg_ref[jnp.where(has_zm, at - 1, at)] == mine)
    same_zp = has_zp & (zagg_ref[jnp.where(has_zp, at + 1, at)] == mine)
    none = jnp.zeros(shape, BF16)

    def settle(pending):
        for j in range(2):
            x, interval, slot = pending[j]
            own = p_ref[layer, :, x].reshape(depth * block, coarse)
            sums_ref[target, interval, slot] += transposed_matmul(own, rows_ref[j])

    def keep(products):
        for y, both in enumerate(products):
            for j in range(2):
                part = both[j * block : (j + 1) * block, j * coarse : (j + 1) * coarse]
                rows_ref[j, y * block : (y + 1) * block] = part.astype(BF16)

    def inner(q, pending):
        settle(pending)
        zm_factor, zp_factor = factor(same_zm, shape), factor(same_zp, shape)
        info = []
        for j in range(2):
            x = 2 * q + j
            has_xm, has_xp = x > 0, x < columns - 1
            before, after = jnp.where(has_xm, x - 1, 0), jnp.where(has_xp, x + 1, x)
            interval = interval_of(xlen_ref, grp, x)
            same_xm = has_xm & (interval_of(xlen_ref, grp, before) == interval)
            same_xp = has_xp & (interval_of(xlen_ref, grp, after) == interval)
            info.append((x, interval, before, after, factor(same_xm, shape), factor(same_xp, shape)))
        products = []
        for y in range(depth):
            stacks = []
            for x, _, before, after, xm_factor, xp_factor in info:
                stacks.append(
                    jnp.concatenate(
                        [
                            p_ref[layer, y, x],
                            p_ref[layer, y, before] * xm_factor,
                            p_ref[layer, y, after] * xp_factor,
                            p_ref[layer, y - 1, x] if y > 0 else none,
                            p_ref[layer, y + 1, x] if y < depth - 1 else none,
                            p_ref[below, y, x] * zm_factor,
                            p_ref[above, y, x] * zp_factor,
                        ],
                        axis=0,
                    )
                )
            left = a_ref[0, y, pl.ds(2 * q, 2)].reshape(2 * block, wide)
            products.append(matmul(left, jnp.concatenate(stacks, axis=1)))
        keep(products)
        return tuple((i[0], i[1], jnp.int32(0)) for i in info)

    def across_x(i, pending):
        settle(pending)
        low, high = aligned(block, 3 * block, wide)
        end = 0
        for n in range(intervals):
            end = end + jnp.where(n <= i, xlen_ref[grp, n], 0)
        x0, x1 = end - 1, end
        products = []
        for y in range(depth):
            stack = jnp.concatenate(
                [
                    jnp.zeros((block - low, 2 * coarse), BF16),
                    jnp.concatenate([none, p_ref[layer, y, x0]], axis=1),
                    jnp.concatenate([p_ref[layer, y, x1], none], axis=1),
                    jnp.zeros((high - 3 * block, 2 * coarse), BF16),
                ],
                axis=0,
            )
            left = jnp.concatenate([a_ref[0, y, x0, :, low:high], a_ref[0, y, x1, :, low:high]], axis=0)
            products.append(matmul(left, stack))
        keep(products)
        return ((x0, i, jnp.int32(2)), (x1, i + 1, jnp.int32(1)))

    def across_z(k, slot, other):
        low, high = aligned(k * block, (k + 1) * block, wide)

        def body(q, pending):
            settle(pending)
            products = []
            for y in range(depth):
                beside = jnp.concatenate([p_ref[other, y, 2 * q + j] for j in range(2)], axis=1)
                left = a_ref[0, y, pl.ds(2 * q, 2), :, low:high].reshape(2 * block, high - low)
                products.append(matmul(left, diagonal([beside], low, k * block, high)))
            keep(products)
            return tuple((2 * q + j, interval_of(xlen_ref, grp, 2 * q + j), jnp.int32(slot)) for j in range(2))

        return body

    zero = jnp.int32(0)
    pending = ((zero, zero, zero), (zero, zero, zero))
    pairs = columns // 2
    pending = lax.fori_loop(0, pairs, inner, pending)
    pending = lax.fori_loop(0, intervals - 1, across_x, pending)
    pairs_zm = jnp.where(has_zm & jnp.logical_not(same_zm), pairs, 0)
    pairs_zp = jnp.where(has_zp & jnp.logical_not(same_zp), pairs, 0)
    pending = lax.fori_loop(0, pairs_zm, across_z(5, 3, below), pending)
    pending = lax.fori_loop(0, pairs_zp, across_z(6, 4, above), pending)
    settle(pending)


def sums_shape(halves, intervals, coarse):
    return jax.ShapeDtypeStruct((halves + 1, intervals, 5, coarse, coarse), F32)


def main(halves, zagg, xlen, a_blocks, prolong):
    layers, depth, columns, block, coarse = prolong.shape
    flops = layers * columns * depth * 2 * block * coarse * 12 * block
    return pl.pallas_call(
        functools.partial(main_kernel, halves),
        grid=(layers,),
        in_specs=[
            scalars(),
            scalars(),
            pl.BlockSpec((1, depth, columns, block, a_blocks.shape[-1]), lambda i: (i, 0, 0, 0, 0)),
            pl.BlockSpec(prolong.shape, lambda i: (0,) * 5, pipeline_mode=pl.Buffered(1)),
        ],
        out_specs=in_vmem(),
        out_shape=sums_shape(halves, xlen.shape[1], coarse),
        scratch_shapes=[pltpu.VMEM((2, depth * block, coarse), BF16)],
        cost_estimate=pl.CostEstimate(flops=flops * 4, bytes_accessed=40 << 20, transcendentals=0),
        compiler_params=pltpu.CompilerParams(vmem_limit_bytes=LIMIT),
        name="coarsen",
    )(zagg, xlen, a_blocks, prolong)


def edge_kernel(halves, zagg_ref, first_ref, last_ref, low_edge_ref, high_edge_ref, left_ref, right_ref, old_ref, sums_ref, early_ref):
    layers, depth, block, coarse = left_ref.shape
    intervals = sums_ref.shape[1]
    dom = lax.axis_index("dom")
    low_first, high_first = aligned(block, 2 * block, 7 * block)
    low_last, high_last = aligned(2 * block, 3 * block, 7 * block)
    none = jnp.zeros((block, coarse), BF16)

    def body(layer, _):
        target = zagg_ref[dom * layers + layer] - dom * halves + 1
        rows = [[], []]
        for y in range(depth):
            first = diagonal([left_ref[layer, y]], low_first, block, high_first)
            last = diagonal([right_ref[layer, y]], low_last, 2 * block, high_last)
            rows[0].append(matmul(first_ref[layer, y, 0], first).astype(BF16))
            rows[1].append(matmul(last_ref[layer, y, 0], last).astype(BF16))
        own = [low_edge_ref[layer].reshape(depth * block, coarse), high_edge_ref[layer].reshape(depth * block, coarse)]
        sums_ref[target, 0, 1] += transposed_matmul(own[0], jnp.concatenate(rows[0], axis=0))
        sums_ref[target, intervals - 1, 2] += transposed_matmul(own[1], jnp.concatenate(rows[1], axis=0))
        return 0

    lax.fori_loop(0, layers, body, 0)

    def emit(i, _):
        for n, slot in enumerate((1, 2, 4)):
            early_ref[n, i] = sums_ref[0, i, slot].astype(BF16)
        return 0

    lax.fori_loop(0, intervals, emit, 0)


def edges(halves, zagg, a_blocks, low_edge, high_edge, left, right, sums):
    layers, depth, columns, block, _ = a_blocks.shape
    intervals, coarse = sums.shape[1], sums.shape[-1]
    lanes = [aligned(k * block, (k + 1) * block, 7 * block)[0] // LANES for k in (1, 2)]
    shape = (layers, depth, 1, block, LANES)
    return pl.pallas_call(
        functools.partial(edge_kernel, halves),
        grid=(1,),
        in_specs=[
            scalars(),
            vmem_block(shape, (0, 0, 0, 0, lanes[0])),
            vmem_block(shape, (0, 0, columns - 1, 0, lanes[1])),
        ]
        + [in_vmem()] * 5,
        out_specs=[in_vmem()] * 2,
        out_shape=[sums, jax.ShapeDtypeStruct((3, intervals, coarse, coarse), BF16)],
        input_output_aliases={7: 0},
        compiler_params=pltpu.CompilerParams(vmem_limit_bytes=LIMIT),
        name="edges",
    )(zagg, a_blocks, a_blocks, low_edge, high_edge, left, right, sums)


def boundary_kernel(zagg_ref, xlen_ref, theirs_ref, pairs_ref, a_ref, p_ref, old_ref, sums_ref, late_ref, upper_ref, lower_ref):
    depth, columns, block, coarse = theirs_ref.shape
    dom, grp = lax.axis_index("dom"), lax.axis_index("grp")
    upper_ref[...] = jnp.zeros_like(upper_ref)
    lower_ref[...] = jnp.zeros_like(lower_ref)
    low, high = aligned(5 * block, 6 * block, 7 * block)

    def upper(q, _):
        rows = [[], []]
        for y in range(depth):
            mine = [p_ref[0, y, 2 * q + j] for j in range(2)]
            both = matmul(pairs_ref[y, q], diagonal(mine, 0, 0, 2 * block))
            for j in range(2):
                rows[j].append(both[:, j * coarse : (j + 1) * coarse].astype(BF16))
        for j in range(2):
            theirs = theirs_ref[:, 2 * q + j].reshape(depth * block, coarse)
            at = interval_of(xlen_ref, grp, 2 * q + j)
            upper_ref[at] += transposed_matmul(theirs, jnp.concatenate(rows[j], axis=0))
        return 0

    def lower(q, _):
        rows = [[], []]
        for y in range(depth):
            theirs = jnp.concatenate([theirs_ref[y, 2 * q + j] for j in range(2)], axis=1)
            left = a_ref[0, y, pl.ds(2 * q, 2)].reshape(2 * block, high - low)
            both = matmul(left, diagonal([theirs], low, 5 * block, high))
            for j in range(2):
                rows[j].append(both[j * block : (j + 1) * block, j * coarse : (j + 1) * coarse].astype(BF16))
        for j in range(2):
            own = p_ref[0, :, 2 * q + j].reshape(depth * block, coarse)
            at = interval_of(xlen_ref, grp, 2 * q + j)
            lower_ref[at] += transposed_matmul(own, jnp.concatenate(rows[j], axis=0))
        return 0

    lax.fori_loop(0, columns // 2, upper, 0)
    lax.fori_loop(0, columns // 2, lower, 0)
    layers = zagg_ref.shape[0] // lax.axis_size("dom")
    at = dom * layers
    same = (at > 0) & (zagg_ref[jnp.where(at > 0, at - 1, 0)] == zagg_ref[at])
    joined = jnp.where(same, 1.0, 0.0)

    def emit(i, _):
        late_ref[i] = (sums_ref[0, i, 0] + upper_ref[i] + joined * lower_ref[i]).astype(BF16)
        sums_ref[1, i, 3] += (1.0 - joined) * lower_ref[i]
        return 0

    lax.fori_loop(0, late_ref.shape[0], emit, 0)


def boundary(zagg, xlen, theirs, pairs, a_blocks, prolong, sums):
    _, depth, columns, block, coarse = prolong.shape
    low, high = aligned(5 * block, 6 * block, 7 * block)
    late = jax.ShapeDtypeStruct((xlen.shape[1], coarse, coarse), BF16)
    return pl.pallas_call(
        boundary_kernel,
        grid=(1,),
        in_specs=[
            scalars(),
            scalars(),
            in_vmem(),
            in_vmem(),
            vmem_block((1, depth, columns, block, high - low), (0, 0, 0, 0, low // LANES)),
            vmem_block((1, depth, columns, block, coarse), (0, 0, 0, 0, 0)),
            in_vmem(),
        ],
        out_specs=[in_vmem()] * 2,
        out_shape=[sums, late],
        scratch_shapes=[pltpu.VMEM(late.shape, F32)] * 2,
        input_output_aliases={6: 0},
        compiler_params=pltpu.CompilerParams(vmem_limit_bytes=LIMIT),
        name="boundary",
    )(zagg, xlen, theirs, pairs, a_blocks, prolong, sums)


def final_kernel(zagg_ref, sums_ref, early_ref, late_ref, out_ref):
    coarse = sums_ref.shape[-1]
    dom = lax.axis_index("dom")
    layers = zagg_ref.shape[0] // lax.axis_size("dom")
    half, halves = pl.program_id(0), pl.num_programs(0)
    last = half == halves - 1
    end = (dom + 1) * layers
    following = jnp.where(end < zagg_ref.shape[0], end, end - 1)
    same = zagg_ref[following] == zagg_ref[end - 1]
    early_factor = jnp.where(last, 1.0, 0.0)
    self_factor = jnp.where(last & same, 1.0, 0.0)
    above_factor = jnp.where(last & jnp.logical_not(same), 1.0, 0.0)

    def body(i, _):
        def put(slot, value):
            out_ref[0, i, :, slot * coarse : (slot + 1) * coarse] = value.astype(BF16)

        late = late_ref[i].astype(F32)
        early = [early_factor * early_ref[n, i].astype(F32) for n in range(3)]
        put(0, sums_ref[half + 1, i, 0] + self_factor * late)
        put(1, sums_ref[half + 1, i, 1] + early[0])
        put(2, sums_ref[half + 1, i, 2] + early[1])
        put(3, sums_ref[half + 1, i, 3])
        put(4, sums_ref[half + 1, i, 4] + early[2] + above_factor * late)
        return 0

    lax.fori_loop(0, out_ref.shape[1], body, 0)


def final(halves, zagg, sums, early, late):
    _, intervals, slots, coarse, _ = sums.shape
    return pl.pallas_call(
        final_kernel,
        grid=(halves,),
        in_specs=[scalars(), in_vmem(), in_vmem(), in_vmem()],
        out_specs=pl.BlockSpec((1, intervals, coarse, slots * coarse), lambda h: (h, 0, 0, 0)),
        out_shape=jax.ShapeDtypeStruct((halves, intervals, coarse, slots * coarse), BF16),
        compiler_params=pltpu.CompilerParams(vmem_limit_bytes=LIMIT),
        name="finish",
    )(zagg, sums, early, late)


def per_device(a_blocks, prolong, zagg, xlen):
    halves = prolong.shape[0] // 2
    prolong = pltpu.with_memory_space_constraint(prolong, pltpu.HBM)
    rows = top(prolong)
    theirs = shifted(rows, "dom", 1)
    pairs, low_edge, high_edge = pack(a_blocks, prolong, rows)
    pairs = shifted(pairs, "dom", 1)
    left = shifted(high_edge, "grp", 1)
    right = shifted(low_edge, "grp", -1)
    sums = main(halves, zagg, xlen, a_blocks, prolong)
    sums, early = edges(halves, zagg, a_blocks, low_edge, high_edge, left, right, sums)
    early = shifted(early, "dom", -1)
    sums, late = boundary(zagg, xlen, theirs, pairs, a_blocks, prolong, sums)
    late = shifted(late, "dom", -1)
    return final(halves, zagg, sums, early, late)


def solution(mesh):
    in_specs = (P("dom", None, "grp", None, None), P("dom", None, "grp", None, None), P(), P())
    out_specs = P("dom", "grp", None, None)
    return jax.shard_map(per_device, mesh=mesh, in_specs=in_specs, out_specs=out_specs, check_vma=False)
```

```python
import functools
import jax
import jax.numpy as jnp
from jax import lax
from jax.experimental import pallas as pl
from jax.experimental.pallas import tpu as pltpu
from jax.sharding import PartitionSpec as P


F32, BF16 = jnp.float32, jnp.bfloat16
LANES = 128
LIMIT = 36 << 20


def vmem_block(shape, index):
    return pl.BlockSpec(shape, lambda *grid: index)


def scalars():
    return pl.BlockSpec(memory_space=pltpu.SMEM)


def in_vmem():
    return pl.BlockSpec(memory_space=pltpu.VMEM)


def shifted(block, axis, distance):
    devices = range(lax.axis_size(axis))
    route = [(i, i + distance) for i in devices if i + distance in devices]
    return lax.ppermute(block, axis, route)


def matmul(left, right):
    return jnp.dot(left, right, preferred_element_type=F32)


def transposed_matmul(left, right):
    return lax.dot_general(left, right, (((0,), (0,)), ((), ())), preferred_element_type=F32)


def interval_of(xlen_ref, group, column):
    end, found = 0, 0
    for i in range(xlen_ref.shape[1]):
        end = end + xlen_ref[group, i]
        found = found + jnp.where(column >= end, 1, 0)
    return found


def aligned(low, high, end):
    return low // LANES * LANES, min(-(-high // LANES) * LANES, end)


def factor(flag, shape):
    return jnp.full(shape, jnp.where(flag, 1.0, 0.0), F32).astype(BF16)


def diagonal(blocks, low, first, high):
    rows, columns = blocks[0].shape
    parts = []
    if first > low:
        parts.append(jnp.zeros((first - low, columns * len(blocks)), BF16))
    none = jnp.zeros((rows, columns), BF16)
    for i, block in enumerate(blocks):
        parts.append(jnp.concatenate([block if i == j else none for j in range(len(blocks))], axis=1))
    end = first + rows * len(blocks)
    if high > end:
        parts.append(jnp.zeros((high - end, columns * len(blocks)), BF16))
    return jnp.concatenate(parts, axis=0)


def top_kernel(p_ref, out_ref, sem):
    copy = pltpu.make_async_copy(p_ref.at[p_ref.shape[0] - 1], out_ref, sem)
    copy.start()
    copy.wait()


def top(prolong):
    return pl.pallas_call(
        top_kernel,
        in_specs=[pl.BlockSpec(memory_space=pltpu.HBM)],
        out_specs=in_vmem(),
        out_shape=jax.ShapeDtypeStruct(prolong.shape[1:], BF16),
        scratch_shapes=[pltpu.SemaphoreType.DMA],
        compiler_params=pltpu.CompilerParams(vmem_limit_bytes=LIMIT),
        name="top",
    )(prolong)


def pack_kernel(a_ref, p_ref, after_ref, pairs_ref, left_ref, right_ref, sems):
    _, depth, block, _ = left_ref.shape
    copies = [
        pltpu.make_async_copy(p_ref.at[:, :, 0], left_ref, sems.at[0]),
        pltpu.make_async_copy(p_ref.at[:, :, p_ref.shape[2] - 1], right_ref, sems.at[1]),
    ]
    for copy in copies:
        copy.start()

    def body(i, _):
        for y in range(depth):
            pair = [a_ref[0, y, 2 * i + j, :, :block] for j in range(2)]
            pairs_ref[y, i] = jnp.concatenate(pair, axis=-1)
        return 0

    lax.fori_loop(0, pairs_ref.shape[1], body, 0)
    for copy in copies:
        copy.wait()


def pack(a_blocks, prolong, after):
    layers, depth, columns, block, coarse = prolong.shape
    low, _ = aligned(6 * block, 7 * block, 7 * block)
    pairs = jax.ShapeDtypeStruct((depth, columns // 2, block, 2 * block), BF16)
    edge = jax.ShapeDtypeStruct((layers, depth, block, coarse), BF16)
    return pl.pallas_call(
        pack_kernel,
        grid=(1,),
        in_specs=[
            vmem_block((1, depth, columns, block, LANES), (layers - 1, 0, 0, 0, low // LANES)),
            pl.BlockSpec(memory_space=pltpu.HBM),
            pl.BlockSpec(memory_space=pl.ANY),
        ],
        out_specs=[in_vmem()] * 3,
        out_shape=[pairs, edge, edge],
        scratch_shapes=[pltpu.SemaphoreType.DMA((2,))],
        compiler_params=pltpu.CompilerParams(vmem_limit_bytes=LIMIT),
        name="pack",
    )(a_blocks, prolong, after)


def main_kernel(halves, zagg_ref, xlen_ref, a_ref, p_ref, sums_ref, bottom_ref, first_ref, last_ref, rows_ref):
    layers, depth, columns, block, coarse = p_ref.shape
    intervals = sums_ref.shape[1]
    wide = a_ref.shape[-1]
    shape = (block, coarse)
    dom, grp = lax.axis_index("dom"), lax.axis_index("grp")
    layer = pl.program_id(0)

    @pl.when(layer == 0)
    def _():
        def clear(i, _):
            for target in range(sums_ref.shape[0]):
                sums_ref[target, i] = jnp.zeros(sums_ref.shape[2:], F32)
            return 0

        lax.fori_loop(0, intervals, clear, 0)

        def bottom(x, _):
            low, high = aligned(5 * block, 6 * block, wide)
            bottom_ref[:, x] = a_ref[0, :, x, :, low:high]
            return 0

        lax.fori_loop(0, columns, bottom, 0)

    low, high = aligned(block, 2 * block, wide)
    first_ref[layer] = a_ref[0, :, 0, :, low:high]
    low, high = aligned(2 * block, 3 * block, wide)
    last_ref[layer] = a_ref[0, :, columns - 1, :, low:high]
    rows_ref[...] = jnp.zeros_like(rows_ref)

    at = dom * layers + layer
    mine = zagg_ref[at]
    target = mine - dom * halves + 1
    has_zm, has_zp = layer > 0, layer < layers - 1
    below = jnp.where(has_zm, layer - 1, 0)
    above = jnp.where(has_zp, layer + 1, layer)
    same_zm = has_zm & (zagg_ref[jnp.where(has_zm, at - 1, at)] == mine)
    same_zp = has_zp & (zagg_ref[jnp.where(has_zp, at + 1, at)] == mine)
    none = jnp.zeros(shape, BF16)

    apart_zm = has_zm & jnp.logical_not(same_zm)
    apart_zp = has_zp & jnp.logical_not(same_zp)
    side = jnp.where(apart_zm, 3, 4)

    def settle(pending):
        for j in range(2):
            x, interval, slot = pending[j]
            own = p_ref[layer, :, x].reshape(depth * block, coarse)
            both = transposed_matmul(own, rows_ref[j])
            sums_ref[target, interval, slot] += both[:, :coarse]
            sums_ref[target, interval, side] += both[:, coarse:]

    def keep(products):
        for y, both in enumerate(products):
            for j in range(2):
                part = both[j * block : (j + 1) * block, j * coarse : (j + 1) * coarse]
                rows_ref[j, y * block : (y + 1) * block, :coarse] = part.astype(BF16)
                rows_ref[j, y * block : (y + 1) * block, coarse:] = none

    def inner(q, pending):
        settle(pending)
        zm_factor, zp_factor = factor(same_zm, shape), factor(same_zp, shape)
        zm_aside = factor(apart_zm, shape)
        zp_aside = factor(apart_zp & jnp.logical_not(apart_zm), shape)
        info = []
        for j in range(2):
            x = 2 * q + j
            has_xm, has_xp = x > 0, x < columns - 1
            before, after = jnp.where(has_xm, x - 1, 0), jnp.where(has_xp, x + 1, x)
            interval = interval_of(xlen_ref, grp, x)
            same_xm = has_xm & (interval_of(xlen_ref, grp, before) == interval)
            same_xp = has_xp & (interval_of(xlen_ref, grp, after) == interval)
            info.append((x, interval, before, after, factor(same_xm, shape), factor(same_xp, shape)))
        products = []
        for j, (x, _, before, after, xm_factor, xp_factor) in enumerate(info):
            for y in range(depth):
                lower, upper = p_ref[below, y, x], p_ref[above, y, x]
                stack = [
                    (p_ref[layer, y, x], none),
                    (p_ref[layer, y, before] * xm_factor, none),
                    (p_ref[layer, y, after] * xp_factor, none),
                    (p_ref[layer, y - 1, x] if y > 0 else none, none),
                    (p_ref[layer, y + 1, x] if y < depth - 1 else none, none),
                    (lower * zm_factor, lower * zm_aside),
                    (upper * zp_factor, upper * zp_aside),
                ]
                stack = jnp.concatenate([jnp.concatenate(row, axis=1) for row in stack], axis=0)
                products.append((j, y, matmul(a_ref[0, y, 2 * q + j], stack)))
        for j, y, both in products:
            rows_ref[j, y * block : (y + 1) * block] = both.astype(BF16)
        return tuple((i[0], i[1], jnp.int32(0)) for i in info)

    def across_x(i, pending):
        settle(pending)
        low, high = aligned(block, 3 * block, wide)
        end = 0
        for n in range(intervals):
            end = end + jnp.where(n <= i, xlen_ref[grp, n], 0)
        x0, x1 = end - 1, end
        products = []
        for y in range(depth):
            stack = jnp.concatenate(
                [
                    jnp.zeros((block - low, 2 * coarse), BF16),
                    jnp.concatenate([none, p_ref[layer, y, x0]], axis=1),
                    jnp.concatenate([p_ref[layer, y, x1], none], axis=1),
                    jnp.zeros((high - 3 * block, 2 * coarse), BF16),
                ],
                axis=0,
            )
            left = jnp.concatenate([a_ref[0, y, x0, :, low:high], a_ref[0, y, x1, :, low:high]], axis=0)
            products.append(matmul(left, stack))
        keep(products)
        return ((x0, i, jnp.int32(2)), (x1, i + 1, jnp.int32(1)))

    def across_z(k, slot, other):
        low, high = aligned(k * block, (k + 1) * block, wide)

        def body(q, pending):
            settle(pending)
            products = []
            for y in range(depth):
                beside = jnp.concatenate([p_ref[other, y, 2 * q + j] for j in range(2)], axis=1)
                left = a_ref[0, y, pl.ds(2 * q, 2), :, low:high].reshape(2 * block, high - low)
                products.append(matmul(left, diagonal([beside], low, k * block, high)))
            keep(products)
            return tuple((2 * q + j, interval_of(xlen_ref, grp, 2 * q + j), jnp.int32(slot)) for j in range(2))

        return body

    zero = jnp.int32(0)
    pending = ((zero, zero, zero), (zero, zero, zero))
    pairs = columns // 2
    pending = lax.fori_loop(0, pairs, inner, pending)
    pending = lax.fori_loop(0, intervals - 1, across_x, pending)
    pairs_zp = jnp.where(apart_zm & apart_zp, pairs, 0)
    pending = lax.fori_loop(0, pairs_zp, across_z(6, 4, above), pending)
    settle(pending)


def sums_shape(halves, intervals, coarse):
    return jax.ShapeDtypeStruct((halves + 1, intervals, 5, coarse, coarse), F32)


def main(halves, zagg, xlen, a_blocks, prolong):
    layers, depth, columns, block, coarse = prolong.shape
    flops = layers * columns * depth * 2 * block * coarse * 12 * block
    return pl.pallas_call(
        functools.partial(main_kernel, halves),
        grid=(layers,),
        in_specs=[
            scalars(),
            scalars(),
            pl.BlockSpec((1, depth, columns, block, a_blocks.shape[-1]), lambda i: (i, 0, 0, 0, 0)),
            in_vmem(),
        ],
        out_specs=[in_vmem()] * 4,
        out_shape=[
            sums_shape(halves, xlen.shape[1], coarse),
            jax.ShapeDtypeStruct((depth, columns, block, LANES), BF16),
            jax.ShapeDtypeStruct((layers, depth, block, LANES), BF16),
            jax.ShapeDtypeStruct((layers, depth, block, LANES), BF16),
        ],
        scratch_shapes=[pltpu.VMEM((2, depth * block, 2 * coarse), BF16)],
        cost_estimate=pl.CostEstimate(flops=flops * 4, bytes_accessed=40 << 20, transcendentals=0),
        compiler_params=pltpu.CompilerParams(vmem_limit_bytes=LIMIT),
        name="coarsen",
    )(zagg, xlen, a_blocks, prolong)


def edge_kernel(halves, zagg_ref, first_ref, last_ref, low_edge_ref, high_edge_ref, left_ref, right_ref, old_ref, sums_ref, early_ref):
    layers, depth, block, coarse = left_ref.shape
    intervals = sums_ref.shape[1]
    dom = lax.axis_index("dom")
    low_first, high_first = aligned(block, 2 * block, 7 * block)
    low_last, high_last = aligned(2 * block, 3 * block, 7 * block)
    none = jnp.zeros((block, coarse), BF16)

    def body(layer, _):
        target = zagg_ref[dom * layers + layer] - dom * halves + 1
        rows = [[], []]
        for y in range(depth):
            first = diagonal([left_ref[layer, y]], low_first, block, high_first)
            last = diagonal([right_ref[layer, y]], low_last, 2 * block, high_last)
            rows[0].append(matmul(first_ref[layer, y], first).astype(BF16))
            rows[1].append(matmul(last_ref[layer, y], last).astype(BF16))
        own = [low_edge_ref[layer].reshape(depth * block, coarse), high_edge_ref[layer].reshape(depth * block, coarse)]
        sums_ref[target, 0, 1] += transposed_matmul(own[0], jnp.concatenate(rows[0], axis=0))
        sums_ref[target, intervals - 1, 2] += transposed_matmul(own[1], jnp.concatenate(rows[1], axis=0))
        return 0

    lax.fori_loop(0, layers, body, 0)

    def emit(i, _):
        for n, slot in enumerate((1, 2, 4)):
            early_ref[n, i] = sums_ref[0, i, slot].astype(BF16)
        return 0

    lax.fori_loop(0, intervals, emit, 0)


def edges(halves, zagg, pieces, low_edge, high_edge, left, right, sums):
    intervals, coarse = sums.shape[1], sums.shape[-1]
    return pl.pallas_call(
        functools.partial(edge_kernel, halves),
        in_specs=[scalars()] + [in_vmem()] * 7,
        out_specs=[in_vmem()] * 2,
        out_shape=[sums, jax.ShapeDtypeStruct((3, intervals, coarse, coarse), BF16)],
        input_output_aliases={7: 0},
        compiler_params=pltpu.CompilerParams(vmem_limit_bytes=LIMIT),
        name="edges",
    )(zagg, *pieces, low_edge, high_edge, left, right, sums)


def lower_kernel(xlen_ref, theirs_ref, a_ref, own_ref, lower_ref):
    depth, columns, block, coarse = theirs_ref.shape
    grp = lax.axis_index("grp")
    lower_ref[...] = jnp.zeros_like(lower_ref)
    low, high = aligned(5 * block, 6 * block, 7 * block)

    group = 2 if columns % 4 == 0 else 1

    def body(step, _):
        rows = []
        for n in range(group):
            q = group * step + n
            parts = [[], []]
            for y in range(depth):
                theirs = jnp.concatenate([theirs_ref[y, 2 * q + j] for j in range(2)], axis=1)
                left = a_ref[y, pl.ds(2 * q, 2)].reshape(2 * block, high - low)
                both = matmul(left, diagonal([theirs], low, 5 * block, high))
                for j in range(2):
                    part = both[j * block : (j + 1) * block, j * coarse : (j + 1) * coarse]
                    parts[j].append(part.astype(BF16))
            rows.extend(jnp.concatenate(part, axis=0) for part in parts)
        for n, right in enumerate(rows):
            x = 2 * group * step + n
            own = own_ref[0, :, x].reshape(depth * block, coarse)
            lower_ref[interval_of(xlen_ref, grp, x)] += transposed_matmul(own, right)
        return 0

    lax.fori_loop(0, columns // (2 * group), body, 0)


def lower_sums(xlen, theirs, bottom, prolong):
    coarse = prolong.shape[-1]
    return pl.pallas_call(
        lower_kernel,
        in_specs=[scalars()] + [in_vmem()] * 3,
        out_specs=in_vmem(),
        out_shape=jax.ShapeDtypeStruct((xlen.shape[1], coarse, coarse), F32),
        compiler_params=pltpu.CompilerParams(vmem_limit_bytes=LIMIT),
        name="lower",
    )(xlen, theirs, bottom, prolong)


def upper_kernel(zagg_ref, xlen_ref, theirs_ref, pairs_ref, own_ref, lower_ref, old_ref, sums_ref, late_ref, upper_ref):
    depth, columns, block, coarse = theirs_ref.shape
    dom, grp = lax.axis_index("dom"), lax.axis_index("grp")
    upper_ref[...] = jnp.zeros_like(upper_ref)
    group = 2 if columns % 4 == 0 else 1

    def body(step, _):
        rows = []
        for n in range(group):
            q = group * step + n
            halves = [[], []]
            for y in range(depth):
                mine = [own_ref[0, y, 2 * q + j] for j in range(2)]
                both = matmul(pairs_ref[y, q], diagonal(mine, 0, 0, 2 * block))
                for j in range(2):
                    halves[j].append(both[:, j * coarse : (j + 1) * coarse].astype(BF16))
            rows.extend(jnp.concatenate(half, axis=0) for half in halves)
        for n, right in enumerate(rows):
            x = 2 * group * step + n
            theirs = theirs_ref[:, x].reshape(depth * block, coarse)
            upper_ref[interval_of(xlen_ref, grp, x)] += transposed_matmul(theirs, right)
        return 0

    lax.fori_loop(0, columns // (2 * group), body, 0)
    layers = zagg_ref.shape[0] // lax.axis_size("dom")
    at = dom * layers
    same = (at > 0) & (zagg_ref[jnp.where(at > 0, at - 1, 0)] == zagg_ref[at])
    joined = jnp.where(same, 1.0, 0.0)

    def emit(i, _):
        late_ref[i] = (sums_ref[0, i, 0] + upper_ref[i] + joined * lower_ref[i]).astype(BF16)
        sums_ref[1, i, 3] += (1.0 - joined) * lower_ref[i]
        return 0

    lax.fori_loop(0, late_ref.shape[0], emit, 0)


def upper_sums(zagg, xlen, theirs, pairs, own, lower, sums):
    late = jax.ShapeDtypeStruct(lower.shape, BF16)
    return pl.pallas_call(
        upper_kernel,
        in_specs=[scalars(), scalars()] + [in_vmem()] * 5,
        out_specs=[in_vmem()] * 2,
        out_shape=[sums, late],
        scratch_shapes=[pltpu.VMEM(late.shape, F32)],
        input_output_aliases={6: 0},
        compiler_params=pltpu.CompilerParams(vmem_limit_bytes=LIMIT),
        name="upper",
    )(zagg, xlen, theirs, pairs, own, lower, sums)


def owned_kernel(sums_ref, out_ref):
    coarse = sums_ref.shape[-1]
    half, i = pl.program_id(0), pl.program_id(1)
    for slot in range(sums_ref.shape[2]):
        out_ref[0, 0, :, slot * coarse : (slot + 1) * coarse] = sums_ref[half + 1, i, slot].astype(BF16)


def last_kernel(zagg_ref, sums_ref, early_ref, late_ref, old_ref, out_ref):
    halves, coarse = sums_ref.shape[0] - 1, sums_ref.shape[-1]
    dom = lax.axis_index("dom")
    end = (dom + 1) * (zagg_ref.shape[0] // lax.axis_size("dom"))
    following = jnp.where(end < zagg_ref.shape[0], end, end - 1)
    self_factor = jnp.where(zagg_ref[following] == zagg_ref[end - 1], 1.0, 0.0)
    i = pl.program_id(0)
    late = late_ref[i].astype(F32)
    more = {
        0: self_factor * late,
        1: early_ref[0, i].astype(F32),
        2: early_ref[1, i].astype(F32),
        4: early_ref[2, i].astype(F32) + (1.0 - self_factor) * late,
    }
    for slot in range(sums_ref.shape[2]):
        value = sums_ref[halves, i, slot]
        value = value + more[slot] if slot in more else value
        out_ref[0, 0, :, slot * coarse : (slot + 1) * coarse] = value.astype(BF16)


def owned(halves, sums):
    _, intervals, slots, coarse, _ = sums.shape
    return pl.pallas_call(
        owned_kernel,
        grid=(halves - 1, intervals),
        in_specs=[in_vmem()],
        out_specs=pl.BlockSpec((1, 1, coarse, slots * coarse), lambda h, i: (h, i, 0, 0)),
        out_shape=jax.ShapeDtypeStruct((halves, intervals, coarse, slots * coarse), BF16),
        compiler_params=pltpu.CompilerParams(vmem_limit_bytes=LIMIT),
        name="owned",
    )(sums)


def last(halves, zagg, sums, early, late, out):
    _, intervals, slots, coarse, _ = sums.shape
    return pl.pallas_call(
        last_kernel,
        grid=(intervals,),
        in_specs=[scalars(), in_vmem(), in_vmem(), in_vmem(), pl.BlockSpec(memory_space=pl.ANY)],
        out_specs=pl.BlockSpec((1, 1, coarse, slots * coarse), lambda i: (halves - 1, i, 0, 0)),
        out_shape=out,
        input_output_aliases={4: 0},
        compiler_params=pltpu.CompilerParams(vmem_limit_bytes=LIMIT),
        name="finish",
    )(zagg, sums, early, late, out)


def per_device(a_blocks, prolong, zagg, xlen):
    halves = prolong.shape[0] // 2
    outside = pltpu.with_memory_space_constraint(prolong, pltpu.HBM)
    rows = top(outside)
    theirs = shifted(rows, "dom", 1)
    pairs, low_edge, high_edge = pack(a_blocks, outside, rows)
    pairs = shifted(pairs, "dom", 1)
    left = shifted(high_edge, "grp", 1)
    right = shifted(low_edge, "grp", -1)
    sums, bottom, *pieces = main(halves, zagg, xlen, a_blocks, prolong)
    sums, early = edges(halves, zagg, pieces, low_edge, high_edge, left, right, sums)
    lower = lower_sums(xlen, theirs, bottom, prolong)
    early = shifted(early, "dom", -1)
    sums, late = upper_sums(zagg, xlen, theirs, pairs, prolong, lower, sums)
    late = shifted(late, "dom", -1)
    return last(halves, zagg, sums, early, late, owned(halves, sums))


def solution(mesh):
    in_specs = (P("dom", None, "grp", None, None), P("dom", None, "grp", None, None), P(), P())
    out_specs = P("dom", "grp", None, None)
    return jax.shard_map(per_device, mesh=mesh, in_specs=in_specs, out_specs=out_specs, check_vma=False)
```

```python
import functools
import jax
import jax.numpy as jnp
from jax import lax
from jax.experimental import pallas as pl
from jax.experimental.pallas import tpu as pltpu
from jax.sharding import PartitionSpec as P


F32, BF16 = jnp.float32, jnp.bfloat16
LANES = 128
LIMIT = 36 << 20


def vmem_block(shape, index):
    return pl.BlockSpec(shape, lambda *grid: index)


def scalars():
    return pl.BlockSpec(memory_space=pltpu.SMEM)


def in_vmem():
    return pl.BlockSpec(memory_space=pltpu.VMEM)


def shifted(block, axis, distance):
    devices = range(lax.axis_size(axis))
    route = [(i, i + distance) for i in devices if i + distance in devices]
    return lax.ppermute(block, axis, route)


def matmul(left, right):
    return jnp.dot(left, right, preferred_element_type=F32)


def transposed_matmul(left, right):
    return lax.dot_general(left, right, (((0,), (0,)), ((), ())), preferred_element_type=F32)


def interval_of(xlen_ref, group, column):
    end, found = 0, 0
    for i in range(xlen_ref.shape[1]):
        end = end + xlen_ref[group, i]
        found = found + jnp.where(column >= end, 1, 0)
    return found


def aligned(low, high, end):
    return low // LANES * LANES, min(-(-high // LANES) * LANES, end)


def factor(flag, shape):
    return jnp.full(shape, jnp.where(flag, 1.0, 0.0), F32).astype(BF16)


def diagonal(blocks, low, first, high):
    rows, columns = blocks[0].shape
    parts = []
    if first > low:
        parts.append(jnp.zeros((first - low, columns * len(blocks)), BF16))
    none = jnp.zeros((rows, columns), BF16)
    for i, block in enumerate(blocks):
        parts.append(jnp.concatenate([block if i == j else none for j in range(len(blocks))], axis=1))
    end = first + rows * len(blocks)
    if high > end:
        parts.append(jnp.zeros((high - end, columns * len(blocks)), BF16))
    return jnp.concatenate(parts, axis=0)


def top_kernel(p_ref, out_ref, sem):
    copy = pltpu.make_async_copy(p_ref.at[p_ref.shape[0] - 1], out_ref, sem)
    copy.start()
    copy.wait()


def top(prolong):
    return pl.pallas_call(
        top_kernel,
        in_specs=[pl.BlockSpec(memory_space=pltpu.HBM)],
        out_specs=in_vmem(),
        out_shape=jax.ShapeDtypeStruct(prolong.shape[1:], BF16),
        scratch_shapes=[pltpu.SemaphoreType.DMA],
        compiler_params=pltpu.CompilerParams(vmem_limit_bytes=LIMIT),
        name="top",
    )(prolong)


def pack_kernel(a_ref, p_ref, after_ref, pairs_ref, left_ref, right_ref, sems):
    _, depth, block, _ = left_ref.shape
    copies = [
        pltpu.make_async_copy(p_ref.at[:, :, 0], left_ref, sems.at[0]),
        pltpu.make_async_copy(p_ref.at[:, :, p_ref.shape[2] - 1], right_ref, sems.at[1]),
    ]
    for copy in copies:
        copy.start()

    def body(i, _):
        for y in range(depth):
            pair = [a_ref[0, y, 2 * i + j, :, :block] for j in range(2)]
            pairs_ref[y, i] = jnp.concatenate(pair, axis=-1)
        return 0

    lax.fori_loop(0, pairs_ref.shape[1], body, 0)
    for copy in copies:
        copy.wait()


def pack(a_blocks, prolong, after):
    layers, depth, columns, block, coarse = prolong.shape
    low, _ = aligned(6 * block, 7 * block, 7 * block)
    pairs = jax.ShapeDtypeStruct((depth, columns // 2, block, 2 * block), BF16)
    edge = jax.ShapeDtypeStruct((layers, depth, block, coarse), BF16)
    return pl.pallas_call(
        pack_kernel,
        grid=(1,),
        in_specs=[
            vmem_block((1, depth, columns, block, LANES), (layers - 1, 0, 0, 0, low // LANES)),
            pl.BlockSpec(memory_space=pltpu.HBM),
            pl.BlockSpec(memory_space=pl.ANY),
        ],
        out_specs=[in_vmem()] * 3,
        out_shape=[pairs, edge, edge],
        scratch_shapes=[pltpu.SemaphoreType.DMA((2,))],
        compiler_params=pltpu.CompilerParams(vmem_limit_bytes=LIMIT),
        name="pack",
    )(a_blocks, prolong, after)


def main_kernel(halves, zagg_ref, xlen_ref, a_ref, p_ref, sums_ref, bottom_ref, first_ref, last_ref, rows_ref):
    layers, depth, columns, block, coarse = p_ref.shape
    intervals = sums_ref.shape[1]
    wide = a_ref.shape[-1]
    shape = (block, coarse)
    dom, grp = lax.axis_index("dom"), lax.axis_index("grp")
    layer = pl.program_id(0)

    @pl.when(layer == 0)
    def _():
        def clear(i, _):
            for target in range(sums_ref.shape[0]):
                sums_ref[target, i] = jnp.zeros(sums_ref.shape[2:], F32)
            return 0

        lax.fori_loop(0, intervals, clear, 0)

        def bottom(x, _):
            low, high = aligned(5 * block, 6 * block, wide)
            bottom_ref[:, x] = a_ref[0, :, x, :, low:high]
            return 0

        lax.fori_loop(0, columns, bottom, 0)

    low, high = aligned(block, 2 * block, wide)
    first_ref[layer] = a_ref[0, :, 0, :, low:high]
    low, high = aligned(2 * block, 3 * block, wide)
    last_ref[layer] = a_ref[0, :, columns - 1, :, low:high]
    rows_ref[...] = jnp.zeros_like(rows_ref)

    at = dom * layers + layer
    mine = zagg_ref[at]
    target = mine - dom * halves + 1
    has_zm, has_zp = layer > 0, layer < layers - 1
    below = jnp.where(has_zm, layer - 1, 0)
    above = jnp.where(has_zp, layer + 1, layer)
    same_zm = has_zm & (zagg_ref[jnp.where(has_zm, at - 1, at)] == mine)
    same_zp = has_zp & (zagg_ref[jnp.where(has_zp, at + 1, at)] == mine)
    none = jnp.zeros(shape, BF16)

    apart_zm = has_zm & jnp.logical_not(same_zm)
    apart_zp = has_zp & jnp.logical_not(same_zp)
    side = jnp.where(apart_zm, 3, 4)

    def settle(pending):
        for j in range(2):
            x, interval, slot = pending[j]
            own = p_ref[layer, :, x].reshape(depth * block, coarse)
            both = transposed_matmul(own, rows_ref[j])
            sums_ref[target, interval, slot] += both[:, :coarse]
            sums_ref[target, interval, side] += both[:, coarse:]

    def keep(products):
        for y, both in enumerate(products):
            for j in range(2):
                part = both[j * block : (j + 1) * block, j * coarse : (j + 1) * coarse]
                rows_ref[j, y * block : (y + 1) * block, :coarse] = part.astype(BF16)
                rows_ref[j, y * block : (y + 1) * block, coarse:] = none

    def inner(q, pending):
        settle(pending)
        zm_factor, zp_factor = factor(same_zm, shape), factor(same_zp, shape)
        zm_aside = factor(apart_zm, shape)
        zp_aside = factor(apart_zp & jnp.logical_not(apart_zm), shape)
        info = []
        for j in range(2):
            x = 2 * q + j
            has_xm, has_xp = x > 0, x < columns - 1
            before, after = jnp.where(has_xm, x - 1, 0), jnp.where(has_xp, x + 1, x)
            interval = interval_of(xlen_ref, grp, x)
            same_xm = has_xm & (interval_of(xlen_ref, grp, before) == interval)
            same_xp = has_xp & (interval_of(xlen_ref, grp, after) == interval)
            info.append((x, interval, before, after, factor(same_xm, shape), factor(same_xp, shape)))
        products = []
        for j, (x, _, before, after, xm_factor, xp_factor) in enumerate(info):
            for y in range(depth):
                lower, upper = p_ref[below, y, x], p_ref[above, y, x]
                stack = [
                    (p_ref[layer, y, x], none),
                    (p_ref[layer, y, before] * xm_factor, none),
                    (p_ref[layer, y, after] * xp_factor, none),
                    (p_ref[layer, y - 1, x] if y > 0 else none, none),
                    (p_ref[layer, y + 1, x] if y < depth - 1 else none, none),
                    (lower * zm_factor, lower * zm_aside),
                    (upper * zp_factor, upper * zp_aside),
                ]
                stack = jnp.concatenate([jnp.concatenate(row, axis=1) for row in stack], axis=0)
                products.append((j, y, matmul(a_ref[0, y, 2 * q + j], stack)))
        for j, y, both in products:
            rows_ref[j, y * block : (y + 1) * block] = both.astype(BF16)
        return tuple((i[0], i[1], jnp.int32(0)) for i in info)

    def across_x(i, pending):
        settle(pending)
        low, high = aligned(block, 3 * block, wide)
        end = 0
        for n in range(intervals):
            end = end + jnp.where(n <= i, xlen_ref[grp, n], 0)
        x0, x1 = end - 1, end
        products = []
        for y in range(depth):
            stack = jnp.concatenate(
                [
                    jnp.zeros((block - low, 2 * coarse), BF16),
                    jnp.concatenate([none, p_ref[layer, y, x0]], axis=1),
                    jnp.concatenate([p_ref[layer, y, x1], none], axis=1),
                    jnp.zeros((high - 3 * block, 2 * coarse), BF16),
                ],
                axis=0,
            )
            left = jnp.concatenate([a_ref[0, y, x0, :, low:high], a_ref[0, y, x1, :, low:high]], axis=0)
            products.append(matmul(left, stack))
        keep(products)
        return ((x0, i, jnp.int32(2)), (x1, i + 1, jnp.int32(1)))

    def across_z(k, slot, other):
        low, high = aligned(k * block, (k + 1) * block, wide)

        def body(q, pending):
            settle(pending)
            products = []
            for y in range(depth):
                beside = jnp.concatenate([p_ref[other, y, 2 * q + j] for j in range(2)], axis=1)
                left = a_ref[0, y, pl.ds(2 * q, 2), :, low:high].reshape(2 * block, high - low)
                products.append(matmul(left, diagonal([beside], low, k * block, high)))
            keep(products)
            return tuple((2 * q + j, interval_of(xlen_ref, grp, 2 * q + j), jnp.int32(slot)) for j in range(2))

        return body

    zero = jnp.int32(0)
    pending = ((zero, zero, zero), (zero, zero, zero))
    pairs = columns // 2
    pending = lax.fori_loop(0, pairs, inner, pending)
    pending = lax.fori_loop(0, intervals - 1, across_x, pending)
    pairs_zp = jnp.where(apart_zm & apart_zp, pairs, 0)
    pending = lax.fori_loop(0, pairs_zp, across_z(6, 4, above), pending)
    settle(pending)


def sums_shape(halves, intervals, coarse):
    return jax.ShapeDtypeStruct((halves + 1, intervals, 5, coarse, coarse), F32)


def main(halves, zagg, xlen, a_blocks, prolong):
    layers, depth, columns, block, coarse = prolong.shape
    flops = layers * columns * depth * 2 * block * coarse * 12 * block
    return pl.pallas_call(
        functools.partial(main_kernel, halves),
        grid=(layers,),
        in_specs=[
            scalars(),
            scalars(),
            pl.BlockSpec((1, depth, columns, block, a_blocks.shape[-1]), lambda i: (i, 0, 0, 0, 0)),
            in_vmem(),
        ],
        out_specs=[in_vmem()] * 4,
        out_shape=[
            sums_shape(halves, xlen.shape[1], coarse),
            jax.ShapeDtypeStruct((depth, columns, block, LANES), BF16),
            jax.ShapeDtypeStruct((layers, depth, block, LANES), BF16),
            jax.ShapeDtypeStruct((layers, depth, block, LANES), BF16),
        ],
        scratch_shapes=[pltpu.VMEM((2, depth * block, 2 * coarse), BF16)],
        cost_estimate=pl.CostEstimate(flops=flops * 4, bytes_accessed=40 << 20, transcendentals=0),
        compiler_params=pltpu.CompilerParams(vmem_limit_bytes=LIMIT),
        name="coarsen",
    )(zagg, xlen, a_blocks, prolong)


def edge_kernel(halves, zagg_ref, first_ref, last_ref, low_edge_ref, high_edge_ref, left_ref, right_ref, old_ref, sums_ref, early_ref):
    layers, depth, block, coarse = left_ref.shape
    intervals = sums_ref.shape[1]
    dom = lax.axis_index("dom")
    low_first, high_first = aligned(block, 2 * block, 7 * block)
    low_last, high_last = aligned(2 * block, 3 * block, 7 * block)
    none = jnp.zeros((block, coarse), BF16)

    def body(layer, _):
        target = zagg_ref[dom * layers + layer] - dom * halves + 1
        rows = [[], []]
        for y in range(depth):
            first = diagonal([left_ref[layer, y]], low_first, block, high_first)
            last = diagonal([right_ref[layer, y]], low_last, 2 * block, high_last)
            rows[0].append(matmul(first_ref[layer, y], first).astype(BF16))
            rows[1].append(matmul(last_ref[layer, y], last).astype(BF16))
        own = [low_edge_ref[layer].reshape(depth * block, coarse), high_edge_ref[layer].reshape(depth * block, coarse)]
        sums_ref[target, 0, 1] += transposed_matmul(own[0], jnp.concatenate(rows[0], axis=0))
        sums_ref[target, intervals - 1, 2] += transposed_matmul(own[1], jnp.concatenate(rows[1], axis=0))
        return 0

    lax.fori_loop(0, layers, body, 0)

    def emit(i, _):
        for n, slot in enumerate((1, 2, 4)):
            early_ref[n, i] = sums_ref[0, i, slot].astype(BF16)
        return 0

    lax.fori_loop(0, intervals, emit, 0)


def edges(halves, zagg, pieces, low_edge, high_edge, left, right, sums):
    intervals, coarse = sums.shape[1], sums.shape[-1]
    return pl.pallas_call(
        functools.partial(edge_kernel, halves),
        in_specs=[scalars()] + [in_vmem()] * 7,
        out_specs=[in_vmem()] * 2,
        out_shape=[sums, jax.ShapeDtypeStruct((3, intervals, coarse, coarse), BF16)],
        input_output_aliases={7: 0},
        compiler_params=pltpu.CompilerParams(vmem_limit_bytes=LIMIT),
        name="edges",
    )(zagg, *pieces, low_edge, high_edge, left, right, sums)


def lower_kernel(xlen_ref, theirs_ref, a_ref, own_ref, lower_ref):
    depth, columns, block, coarse = theirs_ref.shape
    grp = lax.axis_index("grp")
    lower_ref[...] = jnp.zeros_like(lower_ref)
    low, high = aligned(5 * block, 6 * block, 7 * block)

    group = 2 if columns % 4 == 0 else 1

    def body(step, _):
        rows = []
        for n in range(group):
            q = group * step + n
            parts = [[], []]
            for y in range(depth):
                theirs = jnp.concatenate([theirs_ref[y, 2 * q + j] for j in range(2)], axis=1)
                left = a_ref[y, pl.ds(2 * q, 2)].reshape(2 * block, high - low)
                both = matmul(left, diagonal([theirs], low, 5 * block, high))
                for j in range(2):
                    part = both[j * block : (j + 1) * block, j * coarse : (j + 1) * coarse]
                    parts[j].append(part.astype(BF16))
            rows.extend(jnp.concatenate(part, axis=0) for part in parts)
        for n, right in enumerate(rows):
            x = 2 * group * step + n
            own = own_ref[0, :, x].reshape(depth * block, coarse)
            lower_ref[interval_of(xlen_ref, grp, x)] += transposed_matmul(own, right)
        return 0

    lax.fori_loop(0, columns // (2 * group), body, 0)


def lower_sums(xlen, theirs, bottom, prolong):
    coarse = prolong.shape[-1]
    return pl.pallas_call(
        lower_kernel,
        in_specs=[scalars()] + [in_vmem()] * 3,
        out_specs=in_vmem(),
        out_shape=jax.ShapeDtypeStruct((xlen.shape[1], coarse, coarse), F32),
        compiler_params=pltpu.CompilerParams(vmem_limit_bytes=LIMIT),
        name="lower",
    )(xlen, theirs, bottom, prolong)


def upper_kernel(zagg_ref, xlen_ref, theirs_ref, pairs_ref, own_ref, lower_ref, old_ref, sums_ref, late_ref, upper_ref):
    depth, columns, block, coarse = theirs_ref.shape
    dom, grp = lax.axis_index("dom"), lax.axis_index("grp")
    upper_ref[...] = jnp.zeros_like(upper_ref)
    group = 2 if columns % 4 == 0 else 1

    def body(step, _):
        rows = []
        for n in range(group):
            q = group * step + n
            halves = [[], []]
            for y in range(depth):
                mine = [own_ref[0, y, 2 * q + j] for j in range(2)]
                both = matmul(pairs_ref[y, q], diagonal(mine, 0, 0, 2 * block))
                for j in range(2):
                    halves[j].append(both[:, j * coarse : (j + 1) * coarse].astype(BF16))
            rows.extend(jnp.concatenate(half, axis=0) for half in halves)
        for n, right in enumerate(rows):
            x = 2 * group * step + n
            theirs = theirs_ref[:, x].reshape(depth * block, coarse)
            upper_ref[interval_of(xlen_ref, grp, x)] += transposed_matmul(theirs, right)
        return 0

    lax.fori_loop(0, columns // (2 * group), body, 0)
    layers = zagg_ref.shape[0] // lax.axis_size("dom")
    at = dom * layers
    same = (at > 0) & (zagg_ref[jnp.where(at > 0, at - 1, 0)] == zagg_ref[at])
    joined = jnp.where(same, 1.0, 0.0)

    def emit(i, _):
        late_ref[i] = (sums_ref[0, i, 0] + upper_ref[i] + joined * lower_ref[i]).astype(BF16)
        sums_ref[1, i, 3] += (1.0 - joined) * lower_ref[i]
        return 0

    lax.fori_loop(0, late_ref.shape[0], emit, 0)


def upper_sums(zagg, xlen, theirs, pairs, own, lower, sums):
    late = jax.ShapeDtypeStruct(lower.shape, BF16)
    return pl.pallas_call(
        upper_kernel,
        in_specs=[scalars(), scalars()] + [in_vmem()] * 5,
        out_specs=[in_vmem()] * 2,
        out_shape=[sums, late],
        scratch_shapes=[pltpu.VMEM(late.shape, F32)],
        input_output_aliases={6: 0},
        compiler_params=pltpu.CompilerParams(vmem_limit_bytes=LIMIT),
        name="upper",
    )(zagg, xlen, theirs, pairs, own, lower, sums)


def owned_kernel(sums_ref, out_ref):
    coarse = sums_ref.shape[-1]
    half, i = pl.program_id(0), pl.program_id(1)
    for slot in range(sums_ref.shape[2]):
        out_ref[0, 0, :, slot * coarse : (slot + 1) * coarse] = sums_ref[half + 1, i, slot].astype(BF16)


def last_kernel(zagg_ref, sums_ref, early_ref, late_ref, old_ref, out_ref, rows_ref, sems):
    halves, intervals, slots, coarse, _ = sums_ref.shape
    halves = halves - 1
    dom = lax.axis_index("dom")
    end = (dom + 1) * (zagg_ref.shape[0] // lax.axis_size("dom"))
    following = jnp.where(end < zagg_ref.shape[0], end, end - 1)
    self_factor = jnp.where(zagg_ref[following] == zagg_ref[end - 1], 1.0, 0.0)
    copies = []
    for i in range(intervals):
        late = late_ref[i].astype(F32)
        more = {
            0: self_factor * late,
            1: early_ref[0, i].astype(F32),
            2: early_ref[1, i].astype(F32),
            4: early_ref[2, i].astype(F32) + (1.0 - self_factor) * late,
        }
        for slot in range(slots):
            value = sums_ref[halves, i, slot]
            value = value + more[slot] if slot in more else value
            rows_ref[i, :, slot * coarse : (slot + 1) * coarse] = value.astype(BF16)
        copies.append(pltpu.make_async_copy(rows_ref.at[i], out_ref.at[halves - 1, i], sems.at[i]))
        copies[-1].start()
    for copy in copies:
        copy.wait()


def owned(halves, sums):
    _, intervals, slots, coarse, _ = sums.shape
    return pl.pallas_call(
        owned_kernel,
        grid=(halves - 1, intervals),
        in_specs=[in_vmem()],
        out_specs=pl.BlockSpec((1, 1, coarse, slots * coarse), lambda h, i: (h, i, 0, 0)),
        out_shape=jax.ShapeDtypeStruct((halves, intervals, coarse, slots * coarse), BF16),
        compiler_params=pltpu.CompilerParams(vmem_limit_bytes=LIMIT),
        name="owned",
    )(sums)


def last(zagg, sums, early, late, out):
    _, intervals, slots, coarse, _ = sums.shape
    return pl.pallas_call(
        last_kernel,
        in_specs=[scalars(), in_vmem(), in_vmem(), in_vmem(), pl.BlockSpec(memory_space=pltpu.HBM)],
        out_specs=pl.BlockSpec(memory_space=pltpu.HBM),
        out_shape=out,
        scratch_shapes=[
            pltpu.VMEM((intervals, coarse, slots * coarse), BF16),
            pltpu.SemaphoreType.DMA((intervals,)),
        ],
        input_output_aliases={4: 0},
        compiler_params=pltpu.CompilerParams(vmem_limit_bytes=LIMIT),
        name="finish",
    )(zagg, sums, early, late, out)


def per_device(a_blocks, prolong, zagg, xlen):
    halves = prolong.shape[0] // 2
    outside = pltpu.with_memory_space_constraint(prolong, pltpu.HBM)
    rows = top(outside)
    theirs = shifted(rows, "dom", 1)
    pairs, low_edge, high_edge = pack(a_blocks, outside, rows)
    pairs = shifted(pairs, "dom", 1)
    left = shifted(high_edge, "grp", 1)
    right = shifted(low_edge, "grp", -1)
    sums, bottom, *pieces = main(halves, zagg, xlen, a_blocks, prolong)
    sums, early = edges(halves, zagg, pieces, low_edge, high_edge, left, right, sums)
    lower = lower_sums(xlen, theirs, bottom, prolong)
    early = shifted(early, "dom", -1)
    sums, late = upper_sums(zagg, xlen, theirs, pairs, prolong, lower, sums)
    late = shifted(late, "dom", -1)
    return last(zagg, sums, early, late, owned(halves, sums))


def solution(mesh):
    in_specs = (P("dom", None, "grp", None, None), P("dom", None, "grp", None, None), P(), P())
    out_specs = P("dom", "grp", None, None)
    return jax.shard_map(per_device, mesh=mesh, in_specs=in_specs, out_specs=out_specs, check_vma=False)
```

```python
import functools
import jax
import jax.numpy as jnp
from jax import lax
from jax.experimental import pallas as pl
from jax.experimental.pallas import tpu as pltpu
from jax.sharding import PartitionSpec as P


F32, BF16 = jnp.float32, jnp.bfloat16
LANES = 128
LIMIT = 36 << 20


def vmem_block(shape, index):
    return pl.BlockSpec(shape, lambda *grid: index)


def scalars():
    return pl.BlockSpec(memory_space=pltpu.SMEM)


def in_vmem():
    return pl.BlockSpec(memory_space=pltpu.VMEM)


def shifted(block, axis, distance):
    devices = range(lax.axis_size(axis))
    route = [(i, i + distance) for i in devices if i + distance in devices]
    return lax.ppermute(block, axis, route)


def matmul(left, right):
    return jnp.dot(left, right, preferred_element_type=F32)


def transposed_matmul(left, right):
    return lax.dot_general(left, right, (((0,), (0,)), ((), ())), preferred_element_type=F32)


def interval_of(xlen_ref, group, column):
    end, found = 0, 0
    for i in range(xlen_ref.shape[1]):
        end = end + xlen_ref[group, i]
        found = found + jnp.where(column >= end, 1, 0)
    return found


def aligned(low, high, end):
    return low // LANES * LANES, min(-(-high // LANES) * LANES, end)


def group_of(columns):
    return 2 if columns % 4 == 0 else 1


def factor(flag, shape):
    return jnp.full(shape, jnp.where(flag, 1.0, 0.0), F32).astype(BF16)


def diagonal(blocks, low, first, high):
    rows, columns = blocks[0].shape
    parts = []
    if first > low:
        parts.append(jnp.zeros((first - low, columns * len(blocks)), BF16))
    none = jnp.zeros((rows, columns), BF16)
    for i, block in enumerate(blocks):
        parts.append(jnp.concatenate([block if i == j else none for j in range(len(blocks))], axis=1))
    end = first + rows * len(blocks)
    if high > end:
        parts.append(jnp.zeros((high - end, columns * len(blocks)), BF16))
    return jnp.concatenate(parts, axis=0)


def top_kernel(p_ref, out_ref, sem):
    copy = pltpu.make_async_copy(p_ref.at[p_ref.shape[0] - 1], out_ref, sem)
    copy.start()
    copy.wait()


def top(prolong):
    return pl.pallas_call(
        top_kernel,
        in_specs=[pl.BlockSpec(memory_space=pltpu.HBM)],
        out_specs=in_vmem(),
        out_shape=jax.ShapeDtypeStruct(prolong.shape[1:], BF16),
        scratch_shapes=[pltpu.SemaphoreType.DMA],
        compiler_params=pltpu.CompilerParams(vmem_limit_bytes=LIMIT),
        name="top",
    )(prolong)


def pack_kernel(a_ref, p_ref, after_ref, most_ref, rest_ref, left_ref, right_ref, sems):
    _, depth, block, _ = left_ref.shape
    copies = [
        pltpu.make_async_copy(p_ref.at[:, :, 0], left_ref, sems.at[0]),
        pltpu.make_async_copy(p_ref.at[:, :, p_ref.shape[2] - 1], right_ref, sems.at[1]),
    ]
    for copy in copies:
        copy.start()

    most = most_ref.shape[1]
    for first, out_ref in ((0, most_ref), (most, rest_ref)):

        def body(i, _, first=first, out_ref=out_ref):
            for y in range(depth):
                pair = [a_ref[0, y, 2 * (first + i) + j, :, :block] for j in range(2)]
                out_ref[y, i] = jnp.concatenate(pair, axis=-1)
            return 0

        lax.fori_loop(0, out_ref.shape[1], body, 0)
    for copy in copies:
        copy.wait()


def pack(a_blocks, prolong, after):
    layers, depth, columns, block, coarse = prolong.shape
    low, _ = aligned(6 * block, 7 * block, 7 * block)
    rest = group_of(columns)
    pairs = [
        jax.ShapeDtypeStruct((depth, count, block, 2 * block), BF16) for count in (columns // 2 - rest, rest)
    ]
    edge = jax.ShapeDtypeStruct((layers, depth, block, coarse), BF16)
    return pl.pallas_call(
        pack_kernel,
        grid=(1,),
        in_specs=[
            vmem_block((1, depth, columns, block, LANES), (layers - 1, 0, 0, 0, low // LANES)),
            pl.BlockSpec(memory_space=pltpu.HBM),
            pl.BlockSpec(memory_space=pl.ANY),
        ],
        out_specs=[in_vmem()] * 4,
        out_shape=pairs + [edge, edge],
        scratch_shapes=[pltpu.SemaphoreType.DMA((2,))],
        compiler_params=pltpu.CompilerParams(vmem_limit_bytes=LIMIT),
        name="pack",
    )(a_blocks, prolong, after)


def main_kernel(halves, zagg_ref, xlen_ref, a_ref, p_ref, sums_ref, bottom_ref, first_ref, last_ref, rows_ref):
    layers, depth, columns, block, coarse = p_ref.shape
    intervals = sums_ref.shape[1]
    wide = a_ref.shape[-1]
    shape = (block, coarse)
    dom, grp = lax.axis_index("dom"), lax.axis_index("grp")
    layer = pl.program_id(0)

    @pl.when(layer == 0)
    def _():
        def clear(i, _):
            for target in range(sums_ref.shape[0]):
                sums_ref[target, i] = jnp.zeros(sums_ref.shape[2:], F32)
            return 0

        lax.fori_loop(0, intervals, clear, 0)

        def bottom(x, _):
            low, high = aligned(5 * block, 6 * block, wide)
            bottom_ref[:, x] = a_ref[0, :, x, :, low:high]
            return 0

        lax.fori_loop(0, columns, bottom, 0)

    low, high = aligned(block, 2 * block, wide)
    first_ref[layer] = a_ref[0, :, 0, :, low:high]
    low, high = aligned(2 * block, 3 * block, wide)
    last_ref[layer] = a_ref[0, :, columns - 1, :, low:high]
    rows_ref[...] = jnp.zeros_like(rows_ref)

    at = dom * layers + layer
    mine = zagg_ref[at]
    target = mine - dom * halves + 1
    has_zm, has_zp = layer > 0, layer < layers - 1
    below = jnp.where(has_zm, layer - 1, 0)
    above = jnp.where(has_zp, layer + 1, layer)
    same_zm = has_zm & (zagg_ref[jnp.where(has_zm, at - 1, at)] == mine)
    same_zp = has_zp & (zagg_ref[jnp.where(has_zp, at + 1, at)] == mine)
    none = jnp.zeros(shape, BF16)

    apart_zm = has_zm & jnp.logical_not(same_zm)
    apart_zp = has_zp & jnp.logical_not(same_zp)
    side = jnp.where(apart_zm, 3, 4)

    def settle(pending):
        for j in range(2):
            x, interval, slot = pending[j]
            own = p_ref[layer, :, x].reshape(depth * block, coarse)
            both = transposed_matmul(own, rows_ref[j])
            sums_ref[target, interval, slot] += both[:, :coarse]
            sums_ref[target, interval, side] += both[:, coarse:]

    def keep(products):
        for y, both in enumerate(products):
            for j in range(2):
                part = both[j * block : (j + 1) * block, j * coarse : (j + 1) * coarse]
                rows_ref[j, y * block : (y + 1) * block, :coarse] = part.astype(BF16)
                rows_ref[j, y * block : (y + 1) * block, coarse:] = none

    def inner(q, pending):
        settle(pending)
        zm_factor, zp_factor = factor(same_zm, shape), factor(same_zp, shape)
        zm_aside = factor(apart_zm, shape)
        zp_aside = factor(apart_zp & jnp.logical_not(apart_zm), shape)
        info = []
        for j in range(2):
            x = 2 * q + j
            has_xm, has_xp = x > 0, x < columns - 1
            before, after = jnp.where(has_xm, x - 1, 0), jnp.where(has_xp, x + 1, x)
            interval = interval_of(xlen_ref, grp, x)
            same_xm = has_xm & (interval_of(xlen_ref, grp, before) == interval)
            same_xp = has_xp & (interval_of(xlen_ref, grp, after) == interval)
            info.append((x, interval, before, after, factor(same_xm, shape), factor(same_xp, shape)))
        products = []
        for j, (x, _, before, after, xm_factor, xp_factor) in enumerate(info):
            for y in range(depth):
                lower, upper = p_ref[below, y, x], p_ref[above, y, x]
                stack = [
                    (p_ref[layer, y, x], none),
                    (p_ref[layer, y, before] * xm_factor, none),
                    (p_ref[layer, y, after] * xp_factor, none),
                    (p_ref[layer, y - 1, x] if y > 0 else none, none),
                    (p_ref[layer, y + 1, x] if y < depth - 1 else none, none),
                    (lower * zm_factor, lower * zm_aside),
                    (upper * zp_factor, upper * zp_aside),
                ]
                stack = jnp.concatenate([jnp.concatenate(row, axis=1) for row in stack], axis=0)
                products.append((j, y, matmul(a_ref[0, y, 2 * q + j], stack)))
        for j, y, both in products:
            rows_ref[j, y * block : (y + 1) * block] = both.astype(BF16)
        return tuple((i[0], i[1], jnp.int32(0)) for i in info)

    def across_x(i, pending):
        settle(pending)
        low, high = aligned(block, 3 * block, wide)
        end = 0
        for n in range(intervals):
            end = end + jnp.where(n <= i, xlen_ref[grp, n], 0)
        x0, x1 = end - 1, end
        products = []
        for y in range(depth):
            stack = jnp.concatenate(
                [
                    jnp.zeros((block - low, 2 * coarse), BF16),
                    jnp.concatenate([none, p_ref[layer, y, x0]], axis=1),
                    jnp.concatenate([p_ref[layer, y, x1], none], axis=1),
                    jnp.zeros((high - 3 * block, 2 * coarse), BF16),
                ],
                axis=0,
            )
            left = jnp.concatenate([a_ref[0, y, x0, :, low:high], a_ref[0, y, x1, :, low:high]], axis=0)
            products.append(matmul(left, stack))
        keep(products)
        return ((x0, i, jnp.int32(2)), (x1, i + 1, jnp.int32(1)))

    def across_z(k, slot, other):
        low, high = aligned(k * block, (k + 1) * block, wide)

        def body(q, pending):
            settle(pending)
            products = []
            for y in range(depth):
                beside = jnp.concatenate([p_ref[other, y, 2 * q + j] for j in range(2)], axis=1)
                left = a_ref[0, y, pl.ds(2 * q, 2), :, low:high].reshape(2 * block, high - low)
                products.append(matmul(left, diagonal([beside], low, k * block, high)))
            keep(products)
            return tuple((2 * q + j, interval_of(xlen_ref, grp, 2 * q + j), jnp.int32(slot)) for j in range(2))

        return body

    zero = jnp.int32(0)
    pending = ((zero, zero, zero), (zero, zero, zero))
    pairs = columns // 2
    pending = lax.fori_loop(0, pairs, inner, pending)
    pending = lax.fori_loop(0, intervals - 1, across_x, pending)
    pairs_zp = jnp.where(apart_zm & apart_zp, pairs, 0)
    pending = lax.fori_loop(0, pairs_zp, across_z(6, 4, above), pending)
    settle(pending)


def sums_shape(halves, intervals, coarse):
    return jax.ShapeDtypeStruct((halves + 1, intervals, 5, coarse, coarse), F32)


def main(halves, zagg, xlen, a_blocks, prolong):
    layers, depth, columns, block, coarse = prolong.shape
    flops = layers * columns * depth * 2 * block * coarse * 12 * block
    return pl.pallas_call(
        functools.partial(main_kernel, halves),
        grid=(layers,),
        in_specs=[
            scalars(),
            scalars(),
            pl.BlockSpec((1, depth, columns, block, a_blocks.shape[-1]), lambda i: (i, 0, 0, 0, 0)),
            in_vmem(),
        ],
        out_specs=[in_vmem()] * 4,
        out_shape=[
            sums_shape(halves, xlen.shape[1], coarse),
            jax.ShapeDtypeStruct((depth, columns, block, LANES), BF16),
            jax.ShapeDtypeStruct((layers, depth, block, LANES), BF16),
            jax.ShapeDtypeStruct((layers, depth, block, LANES), BF16),
        ],
        scratch_shapes=[pltpu.VMEM((2, depth * block, 2 * coarse), BF16)],
        cost_estimate=pl.CostEstimate(flops=flops * 4, bytes_accessed=40 << 20, transcendentals=0),
        compiler_params=pltpu.CompilerParams(vmem_limit_bytes=LIMIT),
        name="coarsen",
    )(zagg, xlen, a_blocks, prolong)


def edge_kernel(halves, zagg_ref, first_ref, last_ref, low_edge_ref, high_edge_ref, left_ref, right_ref, old_ref, sums_ref, early_ref):
    layers, depth, block, coarse = left_ref.shape
    intervals = sums_ref.shape[1]
    dom = lax.axis_index("dom")
    low_first, high_first = aligned(block, 2 * block, 7 * block)
    low_last, high_last = aligned(2 * block, 3 * block, 7 * block)
    none = jnp.zeros((block, coarse), BF16)

    def body(layer, _):
        target = zagg_ref[dom * layers + layer] - dom * halves + 1
        rows = [[], []]
        for y in range(depth):
            first = diagonal([left_ref[layer, y]], low_first, block, high_first)
            last = diagonal([right_ref[layer, y]], low_last, 2 * block, high_last)
            rows[0].append(matmul(first_ref[layer, y], first).astype(BF16))
            rows[1].append(matmul(last_ref[layer, y], last).astype(BF16))
        own = [low_edge_ref[layer].reshape(depth * block, coarse), high_edge_ref[layer].reshape(depth * block, coarse)]
        sums_ref[target, 0, 1] += transposed_matmul(own[0], jnp.concatenate(rows[0], axis=0))
        sums_ref[target, intervals - 1, 2] += transposed_matmul(own[1], jnp.concatenate(rows[1], axis=0))
        return 0

    lax.fori_loop(0, layers, body, 0)

    def emit(i, _):
        for n, slot in enumerate((1, 2, 4)):
            early_ref[n, i] = sums_ref[0, i, slot].astype(BF16)
        return 0

    lax.fori_loop(0, intervals, emit, 0)


def edges(halves, zagg, pieces, low_edge, high_edge, left, right, sums):
    intervals, coarse = sums.shape[1], sums.shape[-1]
    return pl.pallas_call(
        functools.partial(edge_kernel, halves),
        in_specs=[scalars()] + [in_vmem()] * 7,
        out_specs=[in_vmem()] * 2,
        out_shape=[sums, jax.ShapeDtypeStruct((3, intervals, coarse, coarse), BF16)],
        input_output_aliases={7: 0},
        compiler_params=pltpu.CompilerParams(vmem_limit_bytes=LIMIT),
        name="edges",
    )(zagg, *pieces, low_edge, high_edge, left, right, sums)


def lower_kernel(xlen_ref, theirs_ref, a_ref, own_ref, lower_ref):
    depth, columns, block, coarse = theirs_ref.shape
    grp = lax.axis_index("grp")
    lower_ref[...] = jnp.zeros_like(lower_ref)
    low, high = aligned(5 * block, 6 * block, 7 * block)

    group = group_of(columns)

    def body(step, _):
        rows = []
        for n in range(group):
            q = group * step + n
            parts = [[], []]
            for y in range(depth):
                theirs = jnp.concatenate([theirs_ref[y, 2 * q + j] for j in range(2)], axis=1)
                left = a_ref[y, pl.ds(2 * q, 2)].reshape(2 * block, high - low)
                both = matmul(left, diagonal([theirs], low, 5 * block, high))
                for j in range(2):
                    part = both[j * block : (j + 1) * block, j * coarse : (j + 1) * coarse]
                    parts[j].append(part.astype(BF16))
            rows.extend(jnp.concatenate(part, axis=0) for part in parts)
        for n, right in enumerate(rows):
            x = 2 * group * step + n
            own = own_ref[0, :, x].reshape(depth * block, coarse)
            lower_ref[interval_of(xlen_ref, grp, x)] += transposed_matmul(own, right)
        return 0

    lax.fori_loop(0, columns // (2 * group), body, 0)


def lower_sums(xlen, theirs, bottom, prolong):
    coarse = prolong.shape[-1]
    return pl.pallas_call(
        lower_kernel,
        in_specs=[scalars()] + [in_vmem()] * 3,
        out_specs=in_vmem(),
        out_shape=jax.ShapeDtypeStruct((xlen.shape[1], coarse, coarse), F32),
        compiler_params=pltpu.CompilerParams(vmem_limit_bytes=LIMIT),
        name="lower",
    )(xlen, theirs, bottom, prolong)


def upper_kernel(zagg_ref, xlen_ref, theirs_ref, most_ref, rest_ref, own_ref, lower_ref, old_ref, sums_ref, late_ref, upper_ref):
    depth, columns, block, coarse = theirs_ref.shape
    dom, grp = lax.axis_index("dom"), lax.axis_index("grp")
    upper_ref[...] = jnp.zeros_like(upper_ref)
    group = group_of(columns)

    def body(step, pairs_ref, start):
        rows = []
        for n in range(group):
            q = group * step + n
            halves = [[], []]
            for y in range(depth):
                mine = [own_ref[0, y, 2 * (start + q) + j] for j in range(2)]
                both = matmul(pairs_ref[y, q], diagonal(mine, 0, 0, 2 * block))
                for j in range(2):
                    halves[j].append(both[:, j * coarse : (j + 1) * coarse].astype(BF16))
            rows.extend(jnp.concatenate(half, axis=0) for half in halves)
        for n, right in enumerate(rows):
            x = 2 * (start + group * step) + n
            theirs = theirs_ref[:, x].reshape(depth * block, coarse)
            upper_ref[interval_of(xlen_ref, grp, x)] += transposed_matmul(theirs, right)
        return 0

    most = most_ref.shape[1]
    lax.fori_loop(0, most // group, lambda step, _: body(step, most_ref, 0), 0)
    lax.fori_loop(0, rest_ref.shape[1] // group, lambda step, _: body(step, rest_ref, most), 0)
    layers = zagg_ref.shape[0] // lax.axis_size("dom")
    at = dom * layers
    same = (at > 0) & (zagg_ref[jnp.where(at > 0, at - 1, 0)] == zagg_ref[at])
    joined = jnp.where(same, 1.0, 0.0)

    def emit(i, _):
        late_ref[i] = (sums_ref[0, i, 0] + upper_ref[i] + joined * lower_ref[i]).astype(BF16)
        sums_ref[1, i, 3] += (1.0 - joined) * lower_ref[i]
        return 0

    lax.fori_loop(0, late_ref.shape[0], emit, 0)


def upper_sums(zagg, xlen, theirs, most, rest, own, lower, sums):
    late = jax.ShapeDtypeStruct(lower.shape, BF16)
    return pl.pallas_call(
        upper_kernel,
        in_specs=[scalars(), scalars()] + [in_vmem()] * 6,
        out_specs=[in_vmem()] * 2,
        out_shape=[sums, late],
        scratch_shapes=[pltpu.VMEM(late.shape, F32)],
        input_output_aliases={7: 0},
        compiler_params=pltpu.CompilerParams(vmem_limit_bytes=LIMIT),
        name="upper",
    )(zagg, xlen, theirs, most, rest, own, lower, sums)


def owned_kernel(sums_ref, out_ref):
    coarse = sums_ref.shape[-1]
    half, i = pl.program_id(0), pl.program_id(1)
    for slot in range(sums_ref.shape[2]):
        out_ref[0, 0, :, slot * coarse : (slot + 1) * coarse] = sums_ref[half + 1, i, slot].astype(BF16)


def last_kernel(zagg_ref, sums_ref, early_ref, late_ref, old_ref, out_ref, rows_ref, sems):
    halves, intervals, slots, coarse, _ = sums_ref.shape
    halves = halves - 1
    dom = lax.axis_index("dom")
    end = (dom + 1) * (zagg_ref.shape[0] // lax.axis_size("dom"))
    following = jnp.where(end < zagg_ref.shape[0], end, end - 1)
    self_factor = jnp.where(zagg_ref[following] == zagg_ref[end - 1], 1.0, 0.0)
    copies = []
    for i in range(intervals):
        late = late_ref[i].astype(F32)
        more = {
            0: self_factor * late,
            1: early_ref[0, i].astype(F32),
            2: early_ref[1, i].astype(F32),
            4: early_ref[2, i].astype(F32) + (1.0 - self_factor) * late,
        }
        for slot in range(slots):
            value = sums_ref[halves, i, slot]
            value = value + more[slot] if slot in more else value
            rows_ref[i, :, slot * coarse : (slot + 1) * coarse] = value.astype(BF16)
        copies.append(pltpu.make_async_copy(rows_ref.at[i], out_ref.at[halves - 1, i], sems.at[i]))
        copies[-1].start()
    for copy in copies:
        copy.wait()


def owned(halves, sums):
    _, intervals, slots, coarse, _ = sums.shape
    return pl.pallas_call(
        owned_kernel,
        grid=(halves - 1, intervals),
        in_specs=[in_vmem()],
        out_specs=pl.BlockSpec((1, 1, coarse, slots * coarse), lambda h, i: (h, i, 0, 0)),
        out_shape=jax.ShapeDtypeStruct((halves, intervals, coarse, slots * coarse), BF16),
        compiler_params=pltpu.CompilerParams(vmem_limit_bytes=LIMIT),
        name="owned",
    )(sums)


def last(zagg, sums, early, late, out):
    _, intervals, slots, coarse, _ = sums.shape
    return pl.pallas_call(
        last_kernel,
        in_specs=[scalars(), in_vmem(), in_vmem(), in_vmem(), pl.BlockSpec(memory_space=pltpu.HBM)],
        out_specs=pl.BlockSpec(memory_space=pltpu.HBM),
        out_shape=out,
        scratch_shapes=[
            pltpu.VMEM((intervals, coarse, slots * coarse), BF16),
            pltpu.SemaphoreType.DMA((intervals,)),
        ],
        input_output_aliases={4: 0},
        compiler_params=pltpu.CompilerParams(vmem_limit_bytes=LIMIT),
        name="finish",
    )(zagg, sums, early, late, out)


def per_device(a_blocks, prolong, zagg, xlen):
    halves = prolong.shape[0] // 2
    outside = pltpu.with_memory_space_constraint(prolong, pltpu.HBM)
    rows = top(outside)
    theirs = shifted(rows, "dom", 1)
    most, rest, low_edge, high_edge = pack(a_blocks, outside, rows)
    most = shifted(most, "dom", 1)
    rest = shifted(rest, "dom", 1)
    left = shifted(high_edge, "grp", 1)
    right = shifted(low_edge, "grp", -1)
    sums, bottom, *pieces = main(halves, zagg, xlen, a_blocks, prolong)
    sums, early = edges(halves, zagg, pieces, low_edge, high_edge, left, right, sums)
    lower = lower_sums(xlen, theirs, bottom, prolong)
    early = shifted(early, "dom", -1)
    sums, late = upper_sums(zagg, xlen, theirs, most, rest, prolong, lower, sums)
    late = shifted(late, "dom", -1)
    return last(zagg, sums, early, late, owned(halves, sums))


def solution(mesh):
    in_specs = (P("dom", None, "grp", None, None), P("dom", None, "grp", None, None), P(), P())
    out_specs = P("dom", "grp", None, None)
    return jax.shard_map(per_device, mesh=mesh, in_specs=in_specs, out_specs=out_specs, check_vma=False)
```

```python
import functools
import jax
import jax.numpy as jnp
from jax import lax
from jax.experimental import pallas as pl
from jax.experimental.pallas import tpu as pltpu
from jax.sharding import PartitionSpec as P


F32, BF16 = jnp.float32, jnp.bfloat16
LANES = 128
LIMIT = 36 << 20


def vmem_block(shape, index):
    return pl.BlockSpec(shape, lambda *grid: index)


def scalars():
    return pl.BlockSpec(memory_space=pltpu.SMEM)


def in_vmem():
    return pl.BlockSpec(memory_space=pltpu.VMEM)


def shifted(block, axis, distance):
    devices = range(lax.axis_size(axis))
    route = [(i, i + distance) for i in devices if i + distance in devices]
    return lax.ppermute(block, axis, route)


def matmul(left, right):
    return jnp.dot(left, right, preferred_element_type=F32)


def transposed_matmul(left, right):
    return lax.dot_general(left, right, (((0,), (0,)), ((), ())), preferred_element_type=F32)


def interval_of(xlen_ref, group, column):
    end, found = 0, 0
    for i in range(xlen_ref.shape[1]):
        end = end + xlen_ref[group, i]
        found = found + jnp.where(column >= end, 1, 0)
    return found


def aligned(low, high, end):
    return low // LANES * LANES, min(-(-high // LANES) * LANES, end)


def group_of(columns):
    return 2 if columns % 4 == 0 else 1


def factor(flag, shape):
    return jnp.full(shape, jnp.where(flag, 1.0, 0.0), F32).astype(BF16)


def diagonal(blocks, low, first, high):
    rows, columns = blocks[0].shape
    parts = []
    if first > low:
        parts.append(jnp.zeros((first - low, columns * len(blocks)), BF16))
    none = jnp.zeros((rows, columns), BF16)
    for i, block in enumerate(blocks):
        parts.append(jnp.concatenate([block if i == j else none for j in range(len(blocks))], axis=1))
    end = first + rows * len(blocks)
    if high > end:
        parts.append(jnp.zeros((high - end, columns * len(blocks)), BF16))
    return jnp.concatenate(parts, axis=0)


def top_kernel(p_ref, out_ref, sem):
    copy = pltpu.make_async_copy(p_ref.at[p_ref.shape[0] - 1], out_ref, sem)
    copy.start()
    copy.wait()


def top(prolong):
    return pl.pallas_call(
        top_kernel,
        in_specs=[pl.BlockSpec(memory_space=pltpu.HBM)],
        out_specs=in_vmem(),
        out_shape=jax.ShapeDtypeStruct(prolong.shape[1:], BF16),
        scratch_shapes=[pltpu.SemaphoreType.DMA],
        compiler_params=pltpu.CompilerParams(vmem_limit_bytes=LIMIT),
        name="top",
    )(prolong)


def pack_kernel(a_ref, p_ref, after_ref, most_ref, rest_ref, left_ref, right_ref, sems):
    _, depth, block, _ = left_ref.shape
    copies = [
        pltpu.make_async_copy(p_ref.at[:, :, 0], left_ref, sems.at[0]),
        pltpu.make_async_copy(p_ref.at[:, :, p_ref.shape[2] - 1], right_ref, sems.at[1]),
    ]
    for copy in copies:
        copy.start()

    most = most_ref.shape[1]
    for first, out_ref in ((0, most_ref), (most, rest_ref)):

        def body(i, _, first=first, out_ref=out_ref):
            for y in range(depth):
                pair = [a_ref[0, y, 2 * (first + i) + j, :, :block] for j in range(2)]
                out_ref[y, i] = jnp.concatenate(pair, axis=-1)
            return 0

        lax.fori_loop(0, out_ref.shape[1], body, 0)
    for copy in copies:
        copy.wait()


def pack(a_blocks, prolong, after):
    layers, depth, columns, block, coarse = prolong.shape
    low, _ = aligned(6 * block, 7 * block, 7 * block)
    pairs = [
        jax.ShapeDtypeStruct((depth, count, block, 2 * block), BF16) for count in (columns // 2 - 1, 1)
    ]
    edge = jax.ShapeDtypeStruct((layers, depth, block, coarse), BF16)
    return pl.pallas_call(
        pack_kernel,
        grid=(1,),
        in_specs=[
            vmem_block((1, depth, columns, block, LANES), (layers - 1, 0, 0, 0, low // LANES)),
            pl.BlockSpec(memory_space=pltpu.HBM),
            pl.BlockSpec(memory_space=pl.ANY),
        ],
        out_specs=[in_vmem()] * 4,
        out_shape=pairs + [edge, edge],
        scratch_shapes=[pltpu.SemaphoreType.DMA((2,))],
        compiler_params=pltpu.CompilerParams(vmem_limit_bytes=LIMIT),
        name="pack",
    )(a_blocks, prolong, after)


def main_kernel(halves, zagg_ref, xlen_ref, a_ref, p_ref, sums_ref, bottom_ref, first_ref, last_ref, rows_ref):
    layers, depth, columns, block, coarse = p_ref.shape
    intervals = sums_ref.shape[1]
    wide = a_ref.shape[-1]
    shape = (block, coarse)
    dom, grp = lax.axis_index("dom"), lax.axis_index("grp")
    layer = pl.program_id(0)

    @pl.when(layer == 0)
    def _():
        def clear(i, _):
            for target in range(sums_ref.shape[0]):
                sums_ref[target, i] = jnp.zeros(sums_ref.shape[2:], F32)
            return 0

        lax.fori_loop(0, intervals, clear, 0)

        def bottom(x, _):
            low, high = aligned(5 * block, 6 * block, wide)
            bottom_ref[:, x] = a_ref[0, :, x, :, low:high]
            return 0

        lax.fori_loop(0, columns, bottom, 0)

    low, high = aligned(block, 2 * block, wide)
    first_ref[layer] = a_ref[0, :, 0, :, low:high]
    low, high = aligned(2 * block, 3 * block, wide)
    last_ref[layer] = a_ref[0, :, columns - 1, :, low:high]
    rows_ref[...] = jnp.zeros_like(rows_ref)

    at = dom * layers + layer
    mine = zagg_ref[at]
    target = mine - dom * halves + 1
    has_zm, has_zp = layer > 0, layer < layers - 1
    below = jnp.where(has_zm, layer - 1, 0)
    above = jnp.where(has_zp, layer + 1, layer)
    same_zm = has_zm & (zagg_ref[jnp.where(has_zm, at - 1, at)] == mine)
    same_zp = has_zp & (zagg_ref[jnp.where(has_zp, at + 1, at)] == mine)
    none = jnp.zeros(shape, BF16)

    apart_zm = has_zm & jnp.logical_not(same_zm)
    apart_zp = has_zp & jnp.logical_not(same_zp)
    side = jnp.where(apart_zm, 3, 4)

    def settle(pending):
        for j in range(2):
            x, interval, slot = pending[j]
            own = p_ref[layer, :, x].reshape(depth * block, coarse)
            both = transposed_matmul(own, rows_ref[j])
            sums_ref[target, interval, slot] += both[:, :coarse]
            sums_ref[target, interval, side] += both[:, coarse:]

    def keep(products):
        for y, both in enumerate(products):
            for j in range(2):
                part = both[j * block : (j + 1) * block, j * coarse : (j + 1) * coarse]
                rows_ref[j, y * block : (y + 1) * block, :coarse] = part.astype(BF16)
                rows_ref[j, y * block : (y + 1) * block, coarse:] = none

    def inner(q, pending):
        settle(pending)
        zm_factor, zp_factor = factor(same_zm, shape), factor(same_zp, shape)
        zm_aside = factor(apart_zm, shape)
        zp_aside = factor(apart_zp & jnp.logical_not(apart_zm), shape)
        info = []
        for j in range(2):
            x = 2 * q + j
            has_xm, has_xp = x > 0, x < columns - 1
            before, after = jnp.where(has_xm, x - 1, 0), jnp.where(has_xp, x + 1, x)
            interval = interval_of(xlen_ref, grp, x)
            same_xm = has_xm & (interval_of(xlen_ref, grp, before) == interval)
            same_xp = has_xp & (interval_of(xlen_ref, grp, after) == interval)
            info.append((x, interval, before, after, factor(same_xm, shape), factor(same_xp, shape)))
        products = []
        for j, (x, _, before, after, xm_factor, xp_factor) in enumerate(info):
            for y in range(depth):
                lower, upper = p_ref[below, y, x], p_ref[above, y, x]
                stack = [
                    (p_ref[layer, y, x], none),
                    (p_ref[layer, y, before] * xm_factor, none),
                    (p_ref[layer, y, after] * xp_factor, none),
                    (p_ref[layer, y - 1, x] if y > 0 else none, none),
                    (p_ref[layer, y + 1, x] if y < depth - 1 else none, none),
                    (lower * zm_factor, lower * zm_aside),
                    (upper * zp_factor, upper * zp_aside),
                ]
                stack = jnp.concatenate([jnp.concatenate(row, axis=1) for row in stack], axis=0)
                products.append((j, y, matmul(a_ref[0, y, 2 * q + j], stack)))
        for j, y, both in products:
            rows_ref[j, y * block : (y + 1) * block] = both.astype(BF16)
        return tuple((i[0], i[1], jnp.int32(0)) for i in info)

    def across_x(i, pending):
        settle(pending)
        low, high = aligned(block, 3 * block, wide)
        end = 0
        for n in range(intervals):
            end = end + jnp.where(n <= i, xlen_ref[grp, n], 0)
        x0, x1 = end - 1, end
        products = []
        for y in range(depth):
            stack = jnp.concatenate(
                [
                    jnp.zeros((block - low, 2 * coarse), BF16),
                    jnp.concatenate([none, p_ref[layer, y, x0]], axis=1),
                    jnp.concatenate([p_ref[layer, y, x1], none], axis=1),
                    jnp.zeros((high - 3 * block, 2 * coarse), BF16),
                ],
                axis=0,
            )
            left = jnp.concatenate([a_ref[0, y, x0, :, low:high], a_ref[0, y, x1, :, low:high]], axis=0)
            products.append(matmul(left, stack))
        keep(products)
        return ((x0, i, jnp.int32(2)), (x1, i + 1, jnp.int32(1)))

    def across_z(k, slot, other):
        low, high = aligned(k * block, (k + 1) * block, wide)

        def body(q, pending):
            settle(pending)
            products = []
            for y in range(depth):
                beside = jnp.concatenate([p_ref[other, y, 2 * q + j] for j in range(2)], axis=1)
                left = a_ref[0, y, pl.ds(2 * q, 2), :, low:high].reshape(2 * block, high - low)
                products.append(matmul(left, diagonal([beside], low, k * block, high)))
            keep(products)
            return tuple((2 * q + j, interval_of(xlen_ref, grp, 2 * q + j), jnp.int32(slot)) for j in range(2))

        return body

    zero = jnp.int32(0)
    pending = ((zero, zero, zero), (zero, zero, zero))
    pairs = columns // 2
    pending = lax.fori_loop(0, pairs, inner, pending)
    pending = lax.fori_loop(0, intervals - 1, across_x, pending)
    pairs_zp = jnp.where(apart_zm & apart_zp, pairs, 0)
    pending = lax.fori_loop(0, pairs_zp, across_z(6, 4, above), pending)
    settle(pending)


def sums_shape(halves, intervals, coarse):
    return jax.ShapeDtypeStruct((halves + 1, intervals, 5, coarse, coarse), F32)


def main(halves, zagg, xlen, a_blocks, prolong):
    layers, depth, columns, block, coarse = prolong.shape
    flops = layers * columns * depth * 2 * block * coarse * 12 * block
    return pl.pallas_call(
        functools.partial(main_kernel, halves),
        grid=(layers,),
        in_specs=[
            scalars(),
            scalars(),
            pl.BlockSpec((1, depth, columns, block, a_blocks.shape[-1]), lambda i: (i, 0, 0, 0, 0)),
            in_vmem(),
        ],
        out_specs=[in_vmem()] * 4,
        out_shape=[
            sums_shape(halves, xlen.shape[1], coarse),
            jax.ShapeDtypeStruct((depth, columns, block, LANES), BF16),
            jax.ShapeDtypeStruct((layers, depth, block, LANES), BF16),
            jax.ShapeDtypeStruct((layers, depth, block, LANES), BF16),
        ],
        scratch_shapes=[pltpu.VMEM((2, depth * block, 2 * coarse), BF16)],
        cost_estimate=pl.CostEstimate(flops=flops * 4, bytes_accessed=40 << 20, transcendentals=0),
        compiler_params=pltpu.CompilerParams(vmem_limit_bytes=LIMIT),
        name="coarsen",
    )(zagg, xlen, a_blocks, prolong)


def edge_kernel(halves, zagg_ref, first_ref, last_ref, low_edge_ref, high_edge_ref, left_ref, right_ref, old_ref, sums_ref, early_ref):
    layers, depth, block, coarse = left_ref.shape
    intervals = sums_ref.shape[1]
    dom = lax.axis_index("dom")
    low_first, high_first = aligned(block, 2 * block, 7 * block)
    low_last, high_last = aligned(2 * block, 3 * block, 7 * block)
    none = jnp.zeros((block, coarse), BF16)

    def body(layer, _):
        target = zagg_ref[dom * layers + layer] - dom * halves + 1
        rows = [[], []]
        for y in range(depth):
            first = diagonal([left_ref[layer, y]], low_first, block, high_first)
            last = diagonal([right_ref[layer, y]], low_last, 2 * block, high_last)
            rows[0].append(matmul(first_ref[layer, y], first).astype(BF16))
            rows[1].append(matmul(last_ref[layer, y], last).astype(BF16))
        own = [low_edge_ref[layer].reshape(depth * block, coarse), high_edge_ref[layer].reshape(depth * block, coarse)]
        sums_ref[target, 0, 1] += transposed_matmul(own[0], jnp.concatenate(rows[0], axis=0))
        sums_ref[target, intervals - 1, 2] += transposed_matmul(own[1], jnp.concatenate(rows[1], axis=0))
        return 0

    lax.fori_loop(0, layers, body, 0)

    def emit(i, _):
        for n, slot in enumerate((1, 2, 4)):
            early_ref[n, i] = sums_ref[0, i, slot].astype(BF16)
        return 0

    lax.fori_loop(0, intervals, emit, 0)


def edges(halves, zagg, pieces, low_edge, high_edge, left, right, sums):
    intervals, coarse = sums.shape[1], sums.shape[-1]
    return pl.pallas_call(
        functools.partial(edge_kernel, halves),
        in_specs=[scalars()] + [in_vmem()] * 7,
        out_specs=[in_vmem()] * 2,
        out_shape=[sums, jax.ShapeDtypeStruct((3, intervals, coarse, coarse), BF16)],
        input_output_aliases={7: 0},
        compiler_params=pltpu.CompilerParams(vmem_limit_bytes=LIMIT),
        name="edges",
    )(zagg, *pieces, low_edge, high_edge, left, right, sums)


def lower_kernel(xlen_ref, theirs_ref, a_ref, own_ref, lower_ref):
    depth, columns, block, coarse = theirs_ref.shape
    grp = lax.axis_index("grp")
    lower_ref[...] = jnp.zeros_like(lower_ref)
    low, high = aligned(5 * block, 6 * block, 7 * block)

    group = group_of(columns)

    def body(step, _):
        rows = []
        for n in range(group):
            q = group * step + n
            parts = [[], []]
            for y in range(depth):
                theirs = jnp.concatenate([theirs_ref[y, 2 * q + j] for j in range(2)], axis=1)
                left = a_ref[y, pl.ds(2 * q, 2)].reshape(2 * block, high - low)
                both = matmul(left, diagonal([theirs], low, 5 * block, high))
                for j in range(2):
                    part = both[j * block : (j + 1) * block, j * coarse : (j + 1) * coarse]
                    parts[j].append(part.astype(BF16))
            rows.extend(jnp.concatenate(part, axis=0) for part in parts)
        for n, right in enumerate(rows):
            x = 2 * group * step + n
            own = own_ref[0, :, x].reshape(depth * block, coarse)
            lower_ref[interval_of(xlen_ref, grp, x)] += transposed_matmul(own, right)
        return 0

    lax.fori_loop(0, columns // (2 * group), body, 0)


def lower_sums(xlen, theirs, bottom, prolong):
    coarse = prolong.shape[-1]
    return pl.pallas_call(
        lower_kernel,
        in_specs=[scalars()] + [in_vmem()] * 3,
        out_specs=in_vmem(),
        out_shape=jax.ShapeDtypeStruct((xlen.shape[1], coarse, coarse), F32),
        compiler_params=pltpu.CompilerParams(vmem_limit_bytes=LIMIT),
        name="lower",
    )(xlen, theirs, bottom, prolong)


def upper_kernel(zagg_ref, xlen_ref, theirs_ref, most_ref, rest_ref, own_ref, lower_ref, old_ref, sums_ref, late_ref, upper_ref):
    depth, columns, block, coarse = theirs_ref.shape
    dom, grp = lax.axis_index("dom"), lax.axis_index("grp")
    upper_ref[...] = jnp.zeros_like(upper_ref)
    group = group_of(columns)

    def body(entries):
        rows = []
        for pairs_ref, at, q in entries:
            halves = [[], []]
            for y in range(depth):
                mine = [own_ref[0, y, 2 * q + j] for j in range(2)]
                both = matmul(pairs_ref[y, at], diagonal(mine, 0, 0, 2 * block))
                for j in range(2):
                    halves[j].append(both[:, j * coarse : (j + 1) * coarse].astype(BF16))
            rows.extend((2 * q + j, jnp.concatenate(half, axis=0)) for j, half in enumerate(halves))
        for x, right in rows:
            theirs = theirs_ref[:, x].reshape(depth * block, coarse)
            upper_ref[interval_of(xlen_ref, grp, x)] += transposed_matmul(theirs, right)
        return 0

    most = most_ref.shape[1]
    steps = (most + 1 - group) // group

    def several(step, _):
        return body([(most_ref, group * step + n, group * step + n) for n in range(group)])

    lax.fori_loop(0, steps, several, 0)
    body([(most_ref, q, q) for q in range(group * steps, most)] + [(rest_ref, 0, most)])
    layers = zagg_ref.shape[0] // lax.axis_size("dom")
    at = dom * layers
    same = (at > 0) & (zagg_ref[jnp.where(at > 0, at - 1, 0)] == zagg_ref[at])
    joined = jnp.where(same, 1.0, 0.0)

    def emit(i, _):
        late_ref[i] = (sums_ref[0, i, 0] + upper_ref[i] + joined * lower_ref[i]).astype(BF16)
        sums_ref[1, i, 3] += (1.0 - joined) * lower_ref[i]
        return 0

    lax.fori_loop(0, late_ref.shape[0], emit, 0)


def upper_sums(zagg, xlen, theirs, most, rest, own, lower, sums):
    late = jax.ShapeDtypeStruct(lower.shape, BF16)
    return pl.pallas_call(
        upper_kernel,
        in_specs=[scalars(), scalars()] + [in_vmem()] * 6,
        out_specs=[in_vmem()] * 2,
        out_shape=[sums, late],
        scratch_shapes=[pltpu.VMEM(late.shape, F32)],
        input_output_aliases={7: 0},
        compiler_params=pltpu.CompilerParams(vmem_limit_bytes=LIMIT),
        name="upper",
    )(zagg, xlen, theirs, most, rest, own, lower, sums)


def owned_kernel(sums_ref, out_ref):
    coarse = sums_ref.shape[-1]
    half, i = pl.program_id(0), pl.program_id(1)
    for slot in range(sums_ref.shape[2]):
        out_ref[0, 0, :, slot * coarse : (slot + 1) * coarse] = sums_ref[half + 1, i, slot].astype(BF16)


def last_kernel(zagg_ref, sums_ref, early_ref, late_ref, old_ref, out_ref, rows_ref, sems):
    halves, intervals, slots, coarse, _ = sums_ref.shape
    halves = halves - 1
    dom = lax.axis_index("dom")
    end = (dom + 1) * (zagg_ref.shape[0] // lax.axis_size("dom"))
    following = jnp.where(end < zagg_ref.shape[0], end, end - 1)
    self_factor = jnp.where(zagg_ref[following] == zagg_ref[end - 1], 1.0, 0.0)
    copies = []
    for i in range(intervals):
        late = late_ref[i].astype(F32)
        more = {
            0: self_factor * late,
            1: early_ref[0, i].astype(F32),
            2: early_ref[1, i].astype(F32),
            4: early_ref[2, i].astype(F32) + (1.0 - self_factor) * late,
        }
        for slot in range(slots):
            value = sums_ref[halves, i, slot]
            value = value + more[slot] if slot in more else value
            rows_ref[i, :, slot * coarse : (slot + 1) * coarse] = value.astype(BF16)
        copies.append(pltpu.make_async_copy(rows_ref.at[i], out_ref.at[halves - 1, i], sems.at[i]))
        copies[-1].start()
    for copy in copies:
        copy.wait()


def owned(halves, sums):
    _, intervals, slots, coarse, _ = sums.shape
    return pl.pallas_call(
        owned_kernel,
        grid=(halves - 1, intervals),
        in_specs=[in_vmem()],
        out_specs=pl.BlockSpec((1, 1, coarse, slots * coarse), lambda h, i: (h, i, 0, 0)),
        out_shape=jax.ShapeDtypeStruct((halves, intervals, coarse, slots * coarse), BF16),
        compiler_params=pltpu.CompilerParams(vmem_limit_bytes=LIMIT),
        name="owned",
    )(sums)


def last(zagg, sums, early, late, out):
    _, intervals, slots, coarse, _ = sums.shape
    return pl.pallas_call(
        last_kernel,
        in_specs=[scalars(), in_vmem(), in_vmem(), in_vmem(), pl.BlockSpec(memory_space=pltpu.HBM)],
        out_specs=pl.BlockSpec(memory_space=pltpu.HBM),
        out_shape=out,
        scratch_shapes=[
            pltpu.VMEM((intervals, coarse, slots * coarse), BF16),
            pltpu.SemaphoreType.DMA((intervals,)),
        ],
        input_output_aliases={4: 0},
        compiler_params=pltpu.CompilerParams(vmem_limit_bytes=LIMIT),
        name="finish",
    )(zagg, sums, early, late, out)


def per_device(a_blocks, prolong, zagg, xlen):
    halves = prolong.shape[0] // 2
    outside = pltpu.with_memory_space_constraint(prolong, pltpu.HBM)
    rows = top(outside)
    theirs = shifted(rows, "dom", 1)
    most, rest, low_edge, high_edge = pack(a_blocks, outside, rows)
    most = shifted(most, "dom", 1)
    rest = shifted(rest, "dom", 1)
    left = shifted(high_edge, "grp", 1)
    right = shifted(low_edge, "grp", -1)
    sums, bottom, *pieces = main(halves, zagg, xlen, a_blocks, prolong)
    sums, early = edges(halves, zagg, pieces, low_edge, high_edge, left, right, sums)
    lower = lower_sums(xlen, theirs, bottom, prolong)
    early = shifted(early, "dom", -1)
    sums, late = upper_sums(zagg, xlen, theirs, most, rest, prolong, lower, sums)
    late = shifted(late, "dom", -1)
    return last(zagg, sums, early, late, owned(halves, sums))


def solution(mesh):
    in_specs = (P("dom", None, "grp", None, None), P("dom", None, "grp", None, None), P(), P())
    out_specs = P("dom", "grp", None, None)
    return jax.shard_map(per_device, mesh=mesh, in_specs=in_specs, out_specs=out_specs, check_vma=False)
```

```python
import functools
import jax
import jax.numpy as jnp
from jax import lax
from jax.experimental import pallas as pl
from jax.experimental.pallas import tpu as pltpu
from jax.sharding import PartitionSpec as P


F32, BF16 = jnp.float32, jnp.bfloat16
LANES = 128
LIMIT = 36 << 20


def vmem_block(shape, index):
    return pl.BlockSpec(shape, lambda *grid: index)


def scalars():
    return pl.BlockSpec(memory_space=pltpu.SMEM)


def in_vmem():
    return pl.BlockSpec(memory_space=pltpu.VMEM)


def shifted(block, axis, distance):
    devices = range(lax.axis_size(axis))
    route = [(i, i + distance) for i in devices if i + distance in devices]
    return lax.ppermute(block, axis, route)


def matmul(left, right):
    return jnp.dot(left, right, preferred_element_type=F32)


def transposed_matmul(left, right):
    return lax.dot_general(left, right, (((0,), (0,)), ((), ())), preferred_element_type=F32)


def interval_of(xlen_ref, group, column):
    end, found = 0, 0
    for i in range(xlen_ref.shape[1]):
        end = end + xlen_ref[group, i]
        found = found + jnp.where(column >= end, 1, 0)
    return found


def aligned(low, high, end):
    return low // LANES * LANES, min(-(-high // LANES) * LANES, end)


def group_of(columns):
    return 2 if columns % 4 == 0 else 1


def factor(flag, shape):
    return jnp.full(shape, jnp.where(flag, 1.0, 0.0), F32).astype(BF16)


def diagonal(blocks, low, first, high):
    rows, columns = blocks[0].shape
    parts = []
    if first > low:
        parts.append(jnp.zeros((first - low, columns * len(blocks)), BF16))
    none = jnp.zeros((rows, columns), BF16)
    for i, block in enumerate(blocks):
        parts.append(jnp.concatenate([block if i == j else none for j in range(len(blocks))], axis=1))
    end = first + rows * len(blocks)
    if high > end:
        parts.append(jnp.zeros((high - end, columns * len(blocks)), BF16))
    return jnp.concatenate(parts, axis=0)


def top_kernel(p_ref, out_ref, sems):
    layer = p_ref.shape[0] - 1
    copies = [
        pltpu.make_async_copy(p_ref.at[layer, y], out_ref.at[y], sems.at[y]) for y in range(out_ref.shape[0])
    ]
    for copy in copies:
        copy.start()
    for copy in copies:
        copy.wait()


def top(prolong):
    return pl.pallas_call(
        top_kernel,
        in_specs=[pl.BlockSpec(memory_space=pltpu.HBM)],
        out_specs=in_vmem(),
        out_shape=jax.ShapeDtypeStruct(prolong.shape[1:], BF16),
        scratch_shapes=[pltpu.SemaphoreType.DMA((prolong.shape[1],))],
        compiler_params=pltpu.CompilerParams(vmem_limit_bytes=LIMIT),
        name="top",
    )(prolong)


def pack_kernel(a_ref, p_ref, after_ref, most_ref, rest_ref, left_ref, right_ref, sems):
    _, depth, block, _ = left_ref.shape
    copies = [
        pltpu.make_async_copy(p_ref.at[:, :, 0], left_ref, sems.at[0]),
        pltpu.make_async_copy(p_ref.at[:, :, p_ref.shape[2] - 1], right_ref, sems.at[1]),
    ]
    for copy in copies:
        copy.start()

    most = most_ref.shape[1]
    for first, out_ref in ((0, most_ref), (most, rest_ref)):

        def body(i, _, first=first, out_ref=out_ref):
            for y in range(depth):
                pair = [a_ref[0, y, 2 * (first + i) + j, :, :block] for j in range(2)]
                out_ref[y, i] = jnp.concatenate(pair, axis=-1)
            return 0

        lax.fori_loop(0, out_ref.shape[1], body, 0)
    for copy in copies:
        copy.wait()


def pack(a_blocks, prolong, after):
    layers, depth, columns, block, coarse = prolong.shape
    low, _ = aligned(6 * block, 7 * block, 7 * block)
    pairs = [
        jax.ShapeDtypeStruct((depth, count, block, 2 * block), BF16) for count in (columns // 2 - 1, 1)
    ]
    edge = jax.ShapeDtypeStruct((layers, depth, block, coarse), BF16)
    return pl.pallas_call(
        pack_kernel,
        grid=(1,),
        in_specs=[
            vmem_block((1, depth, columns, block, LANES), (layers - 1, 0, 0, 0, low // LANES)),
            pl.BlockSpec(memory_space=pltpu.HBM),
            pl.BlockSpec(memory_space=pl.ANY),
        ],
        out_specs=[in_vmem()] * 4,
        out_shape=pairs + [edge, edge],
        scratch_shapes=[pltpu.SemaphoreType.DMA((2,))],
        compiler_params=pltpu.CompilerParams(vmem_limit_bytes=LIMIT),
        name="pack",
    )(a_blocks, prolong, after)


def main_kernel(halves, zagg_ref, xlen_ref, a_ref, p_ref, sums_ref, bottom_ref, first_ref, last_ref, rows_ref):
    layers, depth, columns, block, coarse = p_ref.shape
    intervals = sums_ref.shape[1]
    wide = a_ref.shape[-1]
    shape = (block, coarse)
    dom, grp = lax.axis_index("dom"), lax.axis_index("grp")
    layer = pl.program_id(0)

    @pl.when(layer == 0)
    def _():
        def clear(i, _):
            for target in range(sums_ref.shape[0]):
                sums_ref[target, i] = jnp.zeros(sums_ref.shape[2:], F32)
            return 0

        lax.fori_loop(0, intervals, clear, 0)

        def bottom(x, _):
            low, high = aligned(5 * block, 6 * block, wide)
            bottom_ref[:, x] = a_ref[0, :, x, :, low:high]
            return 0

        lax.fori_loop(0, columns, bottom, 0)

    low, high = aligned(block, 2 * block, wide)
    first_ref[layer] = a_ref[0, :, 0, :, low:high]
    low, high = aligned(2 * block, 3 * block, wide)
    last_ref[layer] = a_ref[0, :, columns - 1, :, low:high]
    rows_ref[...] = jnp.zeros_like(rows_ref)

    at = dom * layers + layer
    mine = zagg_ref[at]
    target = mine - dom * halves + 1
    has_zm, has_zp = layer > 0, layer < layers - 1
    below = jnp.where(has_zm, layer - 1, 0)
    above = jnp.where(has_zp, layer + 1, layer)
    same_zm = has_zm & (zagg_ref[jnp.where(has_zm, at - 1, at)] == mine)
    same_zp = has_zp & (zagg_ref[jnp.where(has_zp, at + 1, at)] == mine)
    none = jnp.zeros(shape, BF16)

    apart_zm = has_zm & jnp.logical_not(same_zm)
    apart_zp = has_zp & jnp.logical_not(same_zp)
    side = jnp.where(apart_zm, 3, 4)

    def settle(pending):
        for j in range(2):
            x, interval, slot = pending[j]
            own = p_ref[layer, :, x].reshape(depth * block, coarse)
            both = transposed_matmul(own, rows_ref[j])
            sums_ref[target, interval, slot] += both[:, :coarse]
            sums_ref[target, interval, side] += both[:, coarse:]

    def keep(products):
        for y, both in enumerate(products):
            for j in range(2):
                part = both[j * block : (j + 1) * block, j * coarse : (j + 1) * coarse]
                rows_ref[j, y * block : (y + 1) * block, :coarse] = part.astype(BF16)
                rows_ref[j, y * block : (y + 1) * block, coarse:] = none

    def inner(q, pending):
        settle(pending)
        zm_factor, zp_factor = factor(same_zm, shape), factor(same_zp, shape)
        zm_aside = factor(apart_zm, shape)
        zp_aside = factor(apart_zp & jnp.logical_not(apart_zm), shape)
        info = []
        for j in range(2):
            x = 2 * q + j
            has_xm, has_xp = x > 0, x < columns - 1
            before, after = jnp.where(has_xm, x - 1, 0), jnp.where(has_xp, x + 1, x)
            interval = interval_of(xlen_ref, grp, x)
            same_xm = has_xm & (interval_of(xlen_ref, grp, before) == interval)
            same_xp = has_xp & (interval_of(xlen_ref, grp, after) == interval)
            info.append((x, interval, before, after, factor(same_xm, shape), factor(same_xp, shape)))
        products = []
        for j, (x, _, before, after, xm_factor, xp_factor) in enumerate(info):
            for y in range(depth):
                lower, upper = p_ref[below, y, x], p_ref[above, y, x]
                stack = [
                    (p_ref[layer, y, x], none),
                    (p_ref[layer, y, before] * xm_factor, none),
                    (p_ref[layer, y, after] * xp_factor, none),
                    (p_ref[layer, y - 1, x] if y > 0 else none, none),
                    (p_ref[layer, y + 1, x] if y < depth - 1 else none, none),
                    (lower * zm_factor, lower * zm_aside),
                    (upper * zp_factor, upper * zp_aside),
                ]
                stack = jnp.concatenate([jnp.concatenate(row, axis=1) for row in stack], axis=0)
                products.append((j, y, matmul(a_ref[0, y, 2 * q + j], stack)))
        for j, y, both in products:
            rows_ref[j, y * block : (y + 1) * block] = both.astype(BF16)
        return tuple((i[0], i[1], jnp.int32(0)) for i in info)

    def across_x(i, pending):
        settle(pending)
        low, high = aligned(block, 3 * block, wide)
        end = 0
        for n in range(intervals):
            end = end + jnp.where(n <= i, xlen_ref[grp, n], 0)
        x0, x1 = end - 1, end
        products = []
        for y in range(depth):
            stack = jnp.concatenate(
                [
                    jnp.zeros((block - low, 2 * coarse), BF16),
                    jnp.concatenate([none, p_ref[layer, y, x0]], axis=1),
                    jnp.concatenate([p_ref[layer, y, x1], none], axis=1),
                    jnp.zeros((high - 3 * block, 2 * coarse), BF16),
                ],
                axis=0,
            )
            left = jnp.concatenate([a_ref[0, y, x0, :, low:high], a_ref[0, y, x1, :, low:high]], axis=0)
            products.append(matmul(left, stack))
        keep(products)
        return ((x0, i, jnp.int32(2)), (x1, i + 1, jnp.int32(1)))

    def across_z(k, slot, other):
        low, high = aligned(k * block, (k + 1) * block, wide)

        def body(q, pending):
            settle(pending)
            products = []
            for y in range(depth):
                beside = jnp.concatenate([p_ref[other, y, 2 * q + j] for j in range(2)], axis=1)
                left = a_ref[0, y, pl.ds(2 * q, 2), :, low:high].reshape(2 * block, high - low)
                products.append(matmul(left, diagonal([beside], low, k * block, high)))
            keep(products)
            return tuple((2 * q + j, interval_of(xlen_ref, grp, 2 * q + j), jnp.int32(slot)) for j in range(2))

        return body

    zero = jnp.int32(0)
    pending = ((zero, zero, zero), (zero, zero, zero))
    pairs = columns // 2
    pending = lax.fori_loop(0, pairs, inner, pending)
    pending = lax.fori_loop(0, intervals - 1, across_x, pending)
    pairs_zp = jnp.where(apart_zm & apart_zp, pairs, 0)
    pending = lax.fori_loop(0, pairs_zp, across_z(6, 4, above), pending)
    settle(pending)


def sums_shape(halves, intervals, coarse):
    return jax.ShapeDtypeStruct((halves + 1, intervals, 5, coarse, coarse), F32)


def main(halves, zagg, xlen, a_blocks, prolong):
    layers, depth, columns, block, coarse = prolong.shape
    flops = layers * columns * depth * 2 * block * coarse * 12 * block
    return pl.pallas_call(
        functools.partial(main_kernel, halves),
        grid=(layers,),
        in_specs=[
            scalars(),
            scalars(),
            pl.BlockSpec((1, depth, columns, block, a_blocks.shape[-1]), lambda i: (i, 0, 0, 0, 0)),
            in_vmem(),
        ],
        out_specs=[in_vmem()] * 4,
        out_shape=[
            sums_shape(halves, xlen.shape[1], coarse),
            jax.ShapeDtypeStruct((depth, columns, block, LANES), BF16),
            jax.ShapeDtypeStruct((layers, depth, block, LANES), BF16),
            jax.ShapeDtypeStruct((layers, depth, block, LANES), BF16),
        ],
        scratch_shapes=[pltpu.VMEM((2, depth * block, 2 * coarse), BF16)],
        cost_estimate=pl.CostEstimate(flops=flops * 4, bytes_accessed=40 << 20, transcendentals=0),
        compiler_params=pltpu.CompilerParams(vmem_limit_bytes=LIMIT),
        name="coarsen",
    )(zagg, xlen, a_blocks, prolong)


def edge_kernel(halves, zagg_ref, first_ref, last_ref, low_edge_ref, high_edge_ref, left_ref, right_ref, old_ref, sums_ref, early_ref):
    layers, depth, block, coarse = left_ref.shape
    intervals = sums_ref.shape[1]
    dom = lax.axis_index("dom")
    low_first, high_first = aligned(block, 2 * block, 7 * block)
    low_last, high_last = aligned(2 * block, 3 * block, 7 * block)
    none = jnp.zeros((block, coarse), BF16)

    def body(layer, _):
        target = zagg_ref[dom * layers + layer] - dom * halves + 1
        rows = [[], []]
        for y in range(depth):
            first = diagonal([left_ref[layer, y]], low_first, block, high_first)
            last = diagonal([right_ref[layer, y]], low_last, 2 * block, high_last)
            rows[0].append(matmul(first_ref[layer, y], first).astype(BF16))
            rows[1].append(matmul(last_ref[layer, y], last).astype(BF16))
        own = [low_edge_ref[layer].reshape(depth * block, coarse), high_edge_ref[layer].reshape(depth * block, coarse)]
        sums_ref[target, 0, 1] += transposed_matmul(own[0], jnp.concatenate(rows[0], axis=0))
        sums_ref[target, intervals - 1, 2] += transposed_matmul(own[1], jnp.concatenate(rows[1], axis=0))
        return 0

    lax.fori_loop(0, layers, body, 0)

    def emit(i, _):
        for n, slot in enumerate((1, 2, 4)):
            early_ref[n, i] = sums_ref[0, i, slot].astype(BF16)
        return 0

    lax.fori_loop(0, intervals, emit, 0)


def edges(halves, zagg, pieces, low_edge, high_edge, left, right, sums):
    intervals, coarse = sums.shape[1], sums.shape[-1]
    return pl.pallas_call(
        functools.partial(edge_kernel, halves),
        in_specs=[scalars()] + [in_vmem()] * 7,
        out_specs=[in_vmem()] * 2,
        out_shape=[sums, jax.ShapeDtypeStruct((3, intervals, coarse, coarse), BF16)],
        input_output_aliases={7: 0},
        compiler_params=pltpu.CompilerParams(vmem_limit_bytes=LIMIT),
        name="edges",
    )(zagg, *pieces, low_edge, high_edge, left, right, sums)


def lower_kernel(xlen_ref, theirs_ref, a_ref, own_ref, lower_ref):
    depth, columns, block, coarse = theirs_ref.shape
    grp = lax.axis_index("grp")
    lower_ref[...] = jnp.zeros_like(lower_ref)
    low, high = aligned(5 * block, 6 * block, 7 * block)

    group = group_of(columns)

    def body(step, _):
        rows = []
        for n in range(group):
            q = group * step + n
            parts = [[], []]
            for y in range(depth):
                theirs = jnp.concatenate([theirs_ref[y, 2 * q + j] for j in range(2)], axis=1)
                left = a_ref[y, pl.ds(2 * q, 2)].reshape(2 * block, high - low)
                both = matmul(left, diagonal([theirs], low, 5 * block, high))
                for j in range(2):
                    part = both[j * block : (j + 1) * block, j * coarse : (j + 1) * coarse]
                    parts[j].append(part.astype(BF16))
            rows.extend(jnp.concatenate(part, axis=0) for part in parts)
        for n, right in enumerate(rows):
            x = 2 * group * step + n
            own = own_ref[0, :, x].reshape(depth * block, coarse)
            lower_ref[interval_of(xlen_ref, grp, x)] += transposed_matmul(own, right)
        return 0

    lax.fori_loop(0, columns // (2 * group), body, 0)


def lower_sums(xlen, theirs, bottom, prolong):
    coarse = prolong.shape[-1]
    return pl.pallas_call(
        lower_kernel,
        in_specs=[scalars()] + [in_vmem()] * 3,
        out_specs=in_vmem(),
        out_shape=jax.ShapeDtypeStruct((xlen.shape[1], coarse, coarse), F32),
        compiler_params=pltpu.CompilerParams(vmem_limit_bytes=LIMIT),
        name="lower",
    )(xlen, theirs, bottom, prolong)


def upper_kernel(zagg_ref, xlen_ref, theirs_ref, most_ref, rest_ref, own_ref, lower_ref, old_ref, sums_ref, late_ref, upper_ref):
    depth, columns, block, coarse = theirs_ref.shape
    dom, grp = lax.axis_index("dom"), lax.axis_index("grp")
    upper_ref[...] = jnp.zeros_like(upper_ref)
    group = group_of(columns)

    def body(entries):
        rows = []
        for pairs_ref, at, q in entries:
            halves = [[], []]
            for y in range(depth):
                mine = [own_ref[0, y, 2 * q + j] for j in range(2)]
                both = matmul(pairs_ref[y, at], diagonal(mine, 0, 0, 2 * block))
                for j in range(2):
                    halves[j].append(both[:, j * coarse : (j + 1) * coarse].astype(BF16))
            rows.extend((2 * q + j, jnp.concatenate(half, axis=0)) for j, half in enumerate(halves))
        for x, right in rows:
            theirs = theirs_ref[:, x].reshape(depth * block, coarse)
            upper_ref[interval_of(xlen_ref, grp, x)] += transposed_matmul(theirs, right)
        return 0

    most = most_ref.shape[1]
    steps = (most + 1 - group) // group

    def several(step, _):
        return body([(most_ref, group * step + n, group * step + n) for n in range(group)])

    lax.fori_loop(0, steps, several, 0)
    body([(most_ref, q, q) for q in range(group * steps, most)] + [(rest_ref, 0, most)])
    layers = zagg_ref.shape[0] // lax.axis_size("dom")
    at = dom * layers
    same = (at > 0) & (zagg_ref[jnp.where(at > 0, at - 1, 0)] == zagg_ref[at])
    joined = jnp.where(same, 1.0, 0.0)

    def emit(i, _):
        late_ref[i] = (sums_ref[0, i, 0] + upper_ref[i] + joined * lower_ref[i]).astype(BF16)
        sums_ref[1, i, 3] += (1.0 - joined) * lower_ref[i]
        return 0

    lax.fori_loop(0, late_ref.shape[0], emit, 0)


def upper_sums(zagg, xlen, theirs, most, rest, own, lower, sums):
    late = jax.ShapeDtypeStruct(lower.shape, BF16)
    return pl.pallas_call(
        upper_kernel,
        in_specs=[scalars(), scalars()] + [in_vmem()] * 6,
        out_specs=[in_vmem()] * 2,
        out_shape=[sums, late],
        scratch_shapes=[pltpu.VMEM(late.shape, F32)],
        input_output_aliases={7: 0},
        compiler_params=pltpu.CompilerParams(vmem_limit_bytes=LIMIT),
        name="upper",
    )(zagg, xlen, theirs, most, rest, own, lower, sums)


def owned_kernel(sums_ref, out_ref):
    coarse = sums_ref.shape[-1]
    half, i = pl.program_id(0), pl.program_id(1)
    for slot in range(sums_ref.shape[2]):
        out_ref[0, 0, :, slot * coarse : (slot + 1) * coarse] = sums_ref[half + 1, i, slot].astype(BF16)


def last_kernel(zagg_ref, sums_ref, early_ref, late_ref, old_ref, out_ref, rows_ref, sems):
    halves, intervals, slots, coarse, _ = sums_ref.shape
    halves = halves - 1
    dom = lax.axis_index("dom")
    end = (dom + 1) * (zagg_ref.shape[0] // lax.axis_size("dom"))
    following = jnp.where(end < zagg_ref.shape[0], end, end - 1)
    self_factor = jnp.where(zagg_ref[following] == zagg_ref[end - 1], 1.0, 0.0)
    copies = []
    for i in range(intervals):
        late = late_ref[i].astype(F32)
        more = {
            0: self_factor * late,
            1: early_ref[0, i].astype(F32),
            2: early_ref[1, i].astype(F32),
            4: early_ref[2, i].astype(F32) + (1.0 - self_factor) * late,
        }
        for slot in range(slots):
            value = sums_ref[halves, i, slot]
            value = value + more[slot] if slot in more else value
            rows_ref[i, :, slot * coarse : (slot + 1) * coarse] = value.astype(BF16)
        copies.append(pltpu.make_async_copy(rows_ref.at[i], out_ref.at[halves - 1, i], sems.at[i]))
        copies[-1].start()
    for copy in copies:
        copy.wait()


def owned(halves, sums):
    _, intervals, slots, coarse, _ = sums.shape
    return pl.pallas_call(
        owned_kernel,
        grid=(halves - 1, intervals),
        in_specs=[in_vmem()],
        out_specs=pl.BlockSpec((1, 1, coarse, slots * coarse), lambda h, i: (h, i, 0, 0)),
        out_shape=jax.ShapeDtypeStruct((halves, intervals, coarse, slots * coarse), BF16),
        compiler_params=pltpu.CompilerParams(vmem_limit_bytes=LIMIT),
        name="owned",
    )(sums)


def last(zagg, sums, early, late, out):
    _, intervals, slots, coarse, _ = sums.shape
    return pl.pallas_call(
        last_kernel,
        in_specs=[scalars(), in_vmem(), in_vmem(), in_vmem(), pl.BlockSpec(memory_space=pltpu.HBM)],
        out_specs=pl.BlockSpec(memory_space=pltpu.HBM),
        out_shape=out,
        scratch_shapes=[
            pltpu.VMEM((intervals, coarse, slots * coarse), BF16),
            pltpu.SemaphoreType.DMA((intervals,)),
        ],
        input_output_aliases={4: 0},
        compiler_params=pltpu.CompilerParams(vmem_limit_bytes=LIMIT),
        name="finish",
    )(zagg, sums, early, late, out)


def per_device(a_blocks, prolong, zagg, xlen):
    halves = prolong.shape[0] // 2
    outside = pltpu.with_memory_space_constraint(prolong, pltpu.HBM)
    rows = top(outside)
    theirs = shifted(rows, "dom", 1)
    most, rest, low_edge, high_edge = pack(a_blocks, outside, rows)
    most = shifted(most, "dom", 1)
    rest = shifted(rest, "dom", 1)
    left = shifted(high_edge, "grp", 1)
    right = shifted(low_edge, "grp", -1)
    sums, bottom, *pieces = main(halves, zagg, xlen, a_blocks, prolong)
    sums, early = edges(halves, zagg, pieces, low_edge, high_edge, left, right, sums)
    lower = lower_sums(xlen, theirs, bottom, prolong)
    early = shifted(early, "dom", -1)
    sums, late = upper_sums(zagg, xlen, theirs, most, rest, prolong, lower, sums)
    late = shifted(late, "dom", -1)
    return last(zagg, sums, early, late, owned(halves, sums))


def solution(mesh):
    in_specs = (P("dom", None, "grp", None, None), P("dom", None, "grp", None, None), P(), P())
    out_specs = P("dom", "grp", None, None)
    return jax.shard_map(per_device, mesh=mesh, in_specs=in_specs, out_specs=out_specs, check_vma=False)
```
